256 devices in a mesh: pw: 64 (over y_lo, z, x), atom: 4 (over y_hi, core).
Axes of the slice: x: 4, y: 4 (y_hi: 2, y_lo: 2; y = y_hi * 2 + y_lo), z: 8, core: 2. Of those that a mesh axis runs over, the one named last changes fastest.
Arguments:
- bands_in: float32 [2, 8, 32768], P(None, None, 'pw'), may hold values from -6 to 6
- template: bfloat16 [2, 64, 32768], P(None, None, 'pw'), may hold values from -0.03125 to 0.03125
- potential: bfloat16 [1024, 8192], P(('pw', 'atom')), may hold values from -0.5 to 0.5
- miller: int32 [3, 32768], P(None, 'pw'), may hold values from -32 to 32, as said below
- positions: float32 [3, 1024], replicated, may hold values from 0 to 1
- species: int32 [1024], replicated, may hold values from 0 to 1
- atom_order: int32 [1024], replicated, may hold values from 0 to 1023, each once
- reciprocal: float32 [3], replicated, may hold values from 0.03 to 0.1
Outputs:
- applied_once: float32 [2, 8, 32768], P(None, None, 'pw')
- applied_twice: float32 [2, 8, 32768], P(None, None, 'pw')
The draws below stay inside these ranges and needn't reach their ends.
Inputs may be any that keep to these rules, and one draw needn't show every extreme that they name: `atom_order`: each atom stands in exactly one slot. `miller`: no two plane waves have the same triple of Miller indices; the triples (-32, -32, -32) and (32, 32, 32) are always among them.
All inputs are finite; a program needn't handle non-finite values.
Results may differ from the reference program's by a relative error of at most 0.005.
Values may be sent and summed in bfloat16 or wider, within the bound.
No kernel may reach another device: no remote copies, remote signals or barrier semaphores. Data moves between devices by JAX's collectives and lax.ppermute only.
A program may use at most 64 MiB of HBM per device.

```python
import math
import jax
import jax.numpy as jnp
from jax import lax

LM = 64
BANDS = 8
SPECIES = 2
NPW = 32768
ATOMS = 1024


def draw_miller(key, part):
    side = 65
    cube_count = side * side * side
    flat = jnp.arange(cube_count, dtype=jnp.int32)
    first = flat // (side * side) - 32
    second = flat // side % side - 32
    third = flat % side - 32
    radius_sq = first * first + second * second + third * third
    rank_key = jax.random.fold_in(key, 11)
    ranks = jax.random.permutation(rank_key, cube_count).astype(jnp.int32)
    scores = radius_sq * cube_count + ranks
    scores = jnp.where(flat == 0, jnp.int32(-2), scores)
    scores = jnp.where(flat == cube_count - 1, jnp.int32(-1), scores)
    _, picked = lax.top_k(-scores, NPW)
    picked = picked.astype(jnp.int32)
    shuffle_key = jax.random.fold_in(key, 23)
    picked = picked[jax.random.permutation(shuffle_key, NPW)]
    return jnp.stack([first[picked], second[picked], third[picked]]).astype(jnp.int32)


def touch_ends(drawn, key, smallest, largest):
    extent = drawn.shape
    place = [jax.random.randint(jax.random.fold_in(key, axis), (), 0, extent[axis]) for axis in range(len(extent))]
    drawn = drawn.at[tuple(place)].set(smallest)
    longest = extent.index(max(extent))
    place[longest] = (place[longest] + 1) % extent[longest]
    return drawn.at[tuple(place)].set(largest)


def steps_of(own_key, shape, shards, least, top_value):
    factor_of = 1.0
    for position, parts in shards:
        heights = jax.random.uniform(jax.random.fold_in(jax.random.fold_in(own_key, 6), position), (parts,), jnp.float32, least / len(shards), top_value / len(shards))
        factor_of = factor_of * jnp.repeat(jnp.exp(heights), shape[position] // parts).reshape((-1,) + (1,) * (len(shape) - 1 - position))
    return factor_of


def gaussian(stream_key, shape, scale, bound, cuts=(), held_as=jnp.bfloat16):
    factor_of = steps_of(stream_key, shape, cuts, -0.22, 0.18) if cuts else 1.0
    entries = jax.random.normal(stream_key, shape, jnp.float32) * scale * factor_of
    return jnp.minimum(jnp.maximum(entries, -bound), bound).astype(held_as)


def setup_inputs(seed: int = 0) -> dict:
    streams_of = jax.random.split(jax.random.key(seed), 9)
    return {
        "bands_in": gaussian(streams_of[0], (2, BANDS, NPW), 1.0, 6.0, ((2, 64),), jnp.float32),
        "template": gaussian(streams_of[1], (SPECIES, LM, NPW), NPW ** -0.5, 0.03125, ((2, 64),)),
        "potential": gaussian(streams_of[2], (ATOMS, 2 * LM * LM), (2 * LM) ** -0.5, 0.5, ((0, 256),)),
        "miller": draw_miller(jax.random.fold_in(streams_of[8], 71), 0),
        "positions": jnp.clip(jax.random.uniform(streams_of[4], (3, ATOMS), jnp.float32, 0.0, 1.0), 0.0, 1.0),
        "species": touch_ends(jax.random.randint(streams_of[5], (ATOMS,), 0, SPECIES), jax.random.fold_in(streams_of[5], 1), 0, SPECIES - 1).astype(jnp.int32),
        "atom_order": jax.random.permutation(streams_of[6], ATOMS).astype(jnp.int32),
        "reciprocal": jnp.clip(jnp.exp(jax.random.uniform(streams_of[7], (3,), jnp.float32, math.log(0.03), math.log(0.1))), 0.03, 0.1),
    }


full_turn = 2.0 * math.pi


def phases(miller_real, centres):
    angles = full_turn * (centres[0][:, None] * miller_real[0][None, :] + centres[1][:, None] * miller_real[1][None, :] + centres[2][:, None] * miller_real[2][None, :])
    return jnp.cos(angles), jnp.sin(angles)


def project_block(template_flat, fields, cos_part, sin_part, chosen):
    band_count = fields.shape[1]
    real_wave = cos_part[:, None, :] * fields[0][None] - sin_part[:, None, :] * fields[1][None]
    imag_wave = sin_part[:, None, :] * fields[0][None] + cos_part[:, None, :] * fields[1][None]
    stacked = jnp.stack([real_wave, imag_wave], axis=1).astype(jnp.bfloat16)
    atom_count = stacked.shape[0]
    flattened = stacked.reshape(atom_count * 2 * band_count, stacked.shape[3])
    correlations = lax.dot_general(template_flat, flattened, (((1,), (1,)), ((), ())), preferred_element_type=jnp.float32)
    species_count = chosen.shape[1]
    harmonics = template_flat.shape[0] // species_count
    correlations = correlations.reshape(species_count, harmonics, atom_count, 2, band_count)
    accumulated = jnp.zeros((harmonics, atom_count, 2, band_count), jnp.float32)
    for species_id in range(species_count):
        accumulated = accumulated + chosen[:, species_id][None, :, None, None] * correlations[species_id]
    return jnp.transpose(accumulated, (1, 2, 0, 3))


def product(matrices, vectors):
    return jnp.einsum('alm,amb->alb', matrices, vectors, precision=lax.Precision.HIGHEST)


def apply_potential(potential, coeffs):
    atom_count = coeffs.shape[0]
    harmonics = coeffs.shape[2]
    matrices = potential.astype(jnp.float32).reshape(atom_count, 2, harmonics, harmonics)
    real_new = product(matrices[:, 0], coeffs[:, 0]) - product(matrices[:, 1], coeffs[:, 1])
    imag_new = product(matrices[:, 0], coeffs[:, 1]) + product(matrices[:, 1], coeffs[:, 0])
    return jnp.stack([real_new, imag_new], axis=1).astype(jnp.bfloat16)


def return_block(template_flat, applied, cos_part, sin_part, chosen):
    atom_count, _, harmonics, band_count = applied.shape
    species_count = chosen.shape[1]
    reordered = jnp.transpose(applied, (2, 0, 1, 3))
    selected = jnp.stack([reordered * chosen[:, species_id][None, :, None, None].astype(jnp.bfloat16) for species_id in range(species_count)])
    selected = selected.reshape(species_count * harmonics, atom_count * 2 * band_count)
    images = lax.dot_general(selected, template_flat, (((0,), (0,)), ((), ())), preferred_element_type=jnp.float32)
    images = images.reshape(atom_count, 2, band_count, template_flat.shape[1])
    real_out = jnp.sum(cos_part[:, None, :] * images[:, 0] + sin_part[:, None, :] * images[:, 1], axis=0)
    imag_out = jnp.sum(cos_part[:, None, :] * images[:, 1] - sin_part[:, None, :] * images[:, 0], axis=0)
    return jnp.stack([real_out, imag_out])


def reference(bands_in, template, potential, miller, positions, species, atom_order, reciprocal):
    miller_real = miller.astype(jnp.float32)
    template_flat = template.reshape(SPECIES * LM, NPW)
    kinetic = 0.5 * ((reciprocal[0] * miller_real[0]) ** 2 + (reciprocal[1] * miller_real[1]) ** 2 + (reciprocal[2] * miller_real[2]) ** 2)
    centres = positions[:, atom_order]
    kinds = species[atom_order]
    chosen = (kinds[:, None] == jnp.arange(SPECIES, dtype=jnp.int32)[None, :]).astype(jnp.float32)
    block_size = min(ATOMS, 32)
    block_count = ATOMS // block_size

    def apply_once(fields):
        def projected(blocknum):
            first_row = (blocknum * block_size).astype(jnp.int32)
            centre_part = lax.dynamic_slice_in_dim(centres, first_row, block_size, 1)
            chosen_part = lax.dynamic_slice_in_dim(chosen, first_row, block_size, 0)
            cos_part, sin_part = phases(miller_real, centre_part)
            return project_block(template_flat, fields, cos_part, sin_part, chosen_part)

        coeffs = lax.map(projected, jnp.arange(block_count, dtype=jnp.int32)).reshape(ATOMS, 2, LM, BANDS)
        applied = apply_potential(potential, coeffs)

        def returned(blocknum, summed_up):
            first_row = (blocknum * block_size).astype(jnp.int32)
            centre_part = lax.dynamic_slice_in_dim(centres, first_row, block_size, 1)
            chosen_part = lax.dynamic_slice_in_dim(chosen, first_row, block_size, 0)
            applied_part = lax.dynamic_slice_in_dim(applied, first_row, block_size, 0)
            cos_part, sin_part = phases(miller_real, centre_part)
            return summed_up + return_block(template_flat, applied_part, cos_part, sin_part, chosen_part)

        summed_up = lax.fori_loop(0, block_count, returned, jnp.zeros((2, BANDS, NPW), jnp.float32))
        return summed_up + kinetic[None, None, :] * fields

    applied_once = apply_once(bands_in)
    applied_twice = apply_once(applied_once)
    return applied_once, applied_twice
```

```python
import functools

import jax
import jax.numpy as jnp
from jax import lax
from jax.experimental import pallas as pl
from jax.experimental.pallas import tpu as pltpu
from jax.sharding import PartitionSpec as P

f32 = jnp.float32
bf16 = jnp.bfloat16

COS_TURN = (
    0.9999999890590225,
    -19.739204499453912,
    64.93911745989556,
    -85.45013953088248,
    60.167630950949295,
    -25.96759924849463,
    6.528658161366808,
)
SIN_TURN = (
    6.283185302511503,
    -41.34170040531749,
    81.60513138579344,
    -76.70301535379849,
    42.02592698556796,
    -14.899846667364866,
    3.238137509743233,
)
NT = (((1,), (1,)), ((), ()))
NN = (((1,), (0,)), ((), ()))
CHUNK = 16


def dot(left, right, dims):
    return lax.dot_general(left, right, dims, preferred_element_type=f32)


def horner(coefs, arg):
    total = jnp.full_like(arg, coefs[-1])
    for coef in coefs[-2::-1]:
        total = total * arg + coef
    return total


def three_parts(values):
    high = values.astype(bf16)
    rest = values - high.astype(f32)
    middle = rest.astype(bf16)
    low = (rest - middle.astype(f32)).astype(bf16)
    return high, middle, low


def atom_table(positions, species, order, group, rows, groups, slot_dev):
    atoms = order.shape[1]
    row = lax.broadcasted_iota(jnp.int32, (rows, atoms), 0)
    lane = lax.broadcasted_iota(jnp.int32, (rows, atoms), 1)
    slot = (row // slot_dev * groups + group) * slot_dev + row % slot_dev
    pick_slot = jnp.where(lane == slot, 1.0, 0.0).astype(bf16)
    coarse, fine = order // 128, order % 128
    pad = jnp.zeros((14, atoms), f32)
    digits = jnp.concatenate([coarse.astype(f32), fine.astype(f32), pad], axis=0).astype(bf16)
    found = dot(pick_slot, digits, NT)
    atom = (found[:, 0:1] * 128.0 + found[:, 1:2]).astype(jnp.int32)
    pick_atom = jnp.where(lane == atom, 1.0, 0.0).astype(bf16)
    high, middle, low = three_parts(positions)
    pad = jnp.zeros((6, atoms), bf16)
    facts = jnp.concatenate([high, middle, low, species.astype(f32).astype(bf16), pad], axis=0)
    return dot(pick_atom, facts, NT)


def field_pair(real, imag):
    return jnp.concatenate([real, imag], axis=0), jnp.concatenate([-imag, real], axis=0)


def project_chunk(base, cosine, sine, straight, turned, weights, select, out_ref, wave_ref):
    rows = straight.shape[0]
    for atom in range(CHUNK):
        wave = cosine[atom : atom + 1, :] * straight + sine[atom : atom + 1, :] * turned
        wave_ref[atom * rows : (atom + 1) * rows, :] = wave.astype(bf16)
    both = dot(wave_ref[...], weights, NT)
    low = lax.broadcasted_iota(jnp.int32, (rows, 128), 1) < 64
    for pair in range(CHUNK // 2):
        even = both[2 * pair * rows : (2 * pair + 1) * rows, :]
        odd = both[(2 * pair + 1) * rows : (2 * pair + 2) * rows, :]
        first = jnp.where(low, even[:, :128], odd[:, :128])
        second = jnp.where(low, even[:, 128:], odd[:, 128:])
        mask = select[pair : pair + 1, :]
        chosen = first * mask + second * (1.0 - mask)
        start = pl.multiple_of((base // 2 + pair) * rows, rows)
        out_ref[pl.ds(start, rows), :] = chosen.astype(bf16)


def first_kernel(
    groups, slot_dev, group_ref, bands_ref, template_ref, miller_ref, positions_ref, species_ref,
    order_ref, out_ref, cos_ref, sin_ref, select_ref, table_ref, wave_ref,
):
    atoms = cos_ref.shape[0]
    table_ref[...] = atom_table(
        positions_ref[...], species_ref[...], order_ref[...], group_ref[0], atoms, groups, slot_dev
    )
    miller = miller_ref[...].astype(f32)
    half = bands_ref.shape[0] // 2
    straight, turned = field_pair(bands_ref[:half, :], bands_ref[half:, :])
    template = template_ref[...]
    weights = jnp.concatenate([template, template[64:, :], template[:64, :]], axis=0)
    low = lax.broadcasted_iota(jnp.int32, (CHUNK // 2, 128), 1) < 64

    def step(block, carry):
        base = pl.multiple_of(block * CHUNK, CHUNK)
        table = table_ref[pl.ds(base, CHUNK), :]
        turns = jnp.zeros((CHUNK, miller.shape[1]), f32)
        for axis in range(3):
            centre = table[:, axis : axis + 1] + table[:, 3 + axis : 4 + axis]
            centre = centre + table[:, 6 + axis : 7 + axis]
            turns = turns + centre * miller[axis : axis + 1, :]
        turns = turns - jnp.round(turns)
        square = turns * turns
        cosine = horner(COS_TURN, square)
        sine = turns * horner(SIN_TURN, square)
        cos_ref[pl.ds(base, CHUNK), :] = cosine
        sin_ref[pl.ds(base, CHUNK), :] = sine
        kinds = table[:, 9:10]
        picked = []
        for pair in range(CHUNK // 2):
            even = 1.0 - kinds[2 * pair : 2 * pair + 1, :]
            odd = kinds[2 * pair + 1 : 2 * pair + 2, :]
            picked.append(jnp.where(low[:1, :], even, odd))
        select = jnp.concatenate(picked, axis=0)
        select_ref[pl.ds(pl.multiple_of(block * (CHUNK // 2), CHUNK // 2), CHUNK // 2), :] = select
        project_chunk(base, cosine, sine, straight, turned, weights, select, out_ref, wave_ref)
        return carry

    lax.fori_loop(0, atoms // CHUNK, step, 0)


def kinetic_of(miller, lengths_ref):
    total = jnp.zeros((1, miller.shape[1]), f32)
    for axis in range(3):
        wave_number = lengths_ref[axis] * miller[axis : axis + 1, :]
        total = total + wave_number * wave_number
    return 0.5 * total


def sum_fields(lengths_ref, fields_ref, miller_ref, parts):
    total = kinetic_of(miller_ref[...].astype(f32), lengths_ref) * fields_ref[...]
    own, core, row, both = [part[...] for part in parts]
    return total + ((own + core) + (row + both))


def next_kernel(
    lengths_ref, fields_ref, miller_ref, own_ref, core_ref, row_ref, both_ref, template_ref,
    cos_ref, sin_ref, select_ref, fields_out_ref, out_ref, wave_ref,
):
    atoms = cos_ref.shape[0]
    fields = sum_fields(lengths_ref, fields_ref, miller_ref, (own_ref, core_ref, row_ref, both_ref))
    fields_out_ref[...] = fields
    half = fields.shape[0] // 2
    straight, turned = field_pair(fields[:half, :], fields[half:, :])
    template = template_ref[...]
    weights = jnp.concatenate([template, template[64:, :], template[:64, :]], axis=0)

    def step(block, carry):
        base = pl.multiple_of(block * CHUNK, CHUNK)
        cosine = cos_ref[pl.ds(base, CHUNK), :]
        sine = sin_ref[pl.ds(base, CHUNK), :]
        select = select_ref[pl.ds(pl.multiple_of(block * (CHUNK // 2), CHUNK // 2), CHUNK // 2), :]
        project_chunk(base, cosine, sine, straight, turned, weights, select, out_ref, wave_ref)
        return carry

    lax.fori_loop(0, atoms // CHUNK, step, 0)


def last_kernel(
    lengths_ref, fields_ref, miller_ref, own_ref, core_ref, row_ref, both_ref, fields_out_ref
):
    fields_out_ref[...] = sum_fields(
        lengths_ref, fields_ref, miller_ref, (own_ref, core_ref, row_ref, both_ref)
    )


def potential_kernel(parts_ref, potential_ref, out_ref):
    summed = jnp.sum(parts_ref[...].astype(f32), axis=0)
    pairs = potential_ref.shape[0]
    rows = summed.shape[0] // pairs
    half = rows // 2
    low = lax.broadcasted_iota(jnp.int32, (64, 128), 1) < 64
    results = []
    for pair in range(pairs):
        blocks = []
        for part in range(2):
            matrices = potential_ref[pair, part].astype(f32)
            blocks.append(jnp.where(low, matrices, 0.0))
            blocks.append(jnp.where(low, 0.0, matrices))
        weights = jnp.concatenate(blocks, axis=0).astype(bf16)
        pieces = jnp.concatenate(three_parts(summed[pair * rows : (pair + 1) * rows, :]), axis=0)
        product = dot(pieces, weights, NT)
        product = product[2 * rows :, :] + product[rows : 2 * rows, :] + product[:rows, :]
        real, imag = product[:, :128], product[:, 128:]
        results.append(real[:half, :] - imag[half:, :])
        results.append(real[half:, :] + imag[:half, :])
    applied = jnp.concatenate(results, axis=0).astype(bf16)
    out_ref[...] = jnp.broadcast_to(applied[None], out_ref.shape)


def return_kernel(applied_ref, template_ref, cos_ref, sin_ref, select_ref, out_ref, stack_ref):
    atoms = cos_ref.shape[0]
    rows, waves = out_ref.shape
    half = rows // 2
    template = template_ref[...]
    weights = jnp.concatenate(
        [template[:64, :], template[:64, :], template[64:, :], template[64:, :]], axis=0
    )
    low = jnp.where(lax.broadcasted_iota(jnp.int32, (1, 128), 1) < 64, 1.0, 0.0)

    def step(block, carry):
        straight, turned = carry
        base = pl.multiple_of(block * CHUNK, CHUNK)
        cosine = cos_ref[pl.ds(base, CHUNK), :]
        sine = sin_ref[pl.ds(base, CHUNK), :]
        select = select_ref[pl.ds(pl.multiple_of(block * (CHUNK // 2), CHUNK // 2), CHUNK // 2), :]
        for pair in range(CHUNK // 2):
            start = pl.multiple_of((base // 2 + pair) * rows, rows)
            applied = applied_ref[pl.ds(start, rows), :].astype(f32)
            mask = select[pair : pair + 1, :]
            is_first = low * mask + (1.0 - low) * (1.0 - mask)
            kept, other = applied * is_first, applied * (1.0 - is_first)
            top = slice(2 * pair * rows, (2 * pair + 1) * rows)
            bottom = slice((2 * pair + 1) * rows, (2 * pair + 2) * rows)
            stack_ref[top, :128] = (kept * low).astype(bf16)
            stack_ref[top, 128:] = (other * low).astype(bf16)
            stack_ref[bottom, :128] = (kept * (1.0 - low)).astype(bf16)
            stack_ref[bottom, 128:] = (other * (1.0 - low)).astype(bf16)
        images = dot(stack_ref[...], weights, NN)
        for atom in range(CHUNK):
            image = images[atom * rows : (atom + 1) * rows, :]
            straight = straight + cosine[atom : atom + 1, :] * image
            turned = turned + sine[atom : atom + 1, :] * image
        return straight, turned

    zero = jnp.zeros((rows, waves), f32)
    straight, turned = lax.fori_loop(0, atoms // CHUNK, step, (zero, zero))
    out_ref[:half, :] = straight[:half, :] + turned[half:, :]
    out_ref[half:, :] = straight[half:, :] - turned[:half, :]


def vmem(count):
    return [pl.BlockSpec(memory_space=pltpu.VMEM)] * count


def smem(count):
    return [pl.BlockSpec(memory_space=pltpu.SMEM)] * count


def shape(dims, dtype):
    return jax.ShapeDtypeStruct(dims, dtype)


def per_device(bands_in, template, potential, miller, positions, species, atom_order, reciprocal):
    pw_count = lax.axis_size("pw")
    group_count = lax.axis_size("atom")
    slot_dev = potential.shape[0]
    atoms = slot_dev * pw_count
    species_count, harmonics, waves = template.shape
    rows = 2 * bands_in.shape[1]
    pairs = slot_dev // 2
    message = pairs * rows
    template = template.reshape(species_count * harmonics, waves)
    fields = bands_in.reshape(rows, waves)
    matrices = potential.reshape(pairs, 2, 2, harmonics, harmonics)
    matrices = matrices.transpose(0, 2, 3, 1, 4).reshape(pairs, 2, harmonics, 2 * harmonics)
    group = lax.axis_index("atom").astype(jnp.int32).reshape(1)
    coefs_shape = shape((atoms // 2 * rows, 2 * harmonics), bf16)
    fields_shape = shape((rows, waves), f32)
    phase_shape = shape((atoms, waves), f32)
    wave_scratch = pltpu.VMEM((CHUNK * rows, waves), bf16)

    coefs, cosine, sine, select = pl.pallas_call(
        functools.partial(first_kernel, group_count, slot_dev),
        in_specs=smem(1) + vmem(6),
        out_specs=tuple(vmem(4)),
        out_shape=(coefs_shape, phase_shape, phase_shape, shape((atoms // 2, 128), f32)),
        scratch_shapes=[pltpu.VMEM((atoms, 16), f32), wave_scratch],
        name="first",
    )(group, fields, template, miller, positions, species.reshape(1, -1), atom_order.reshape(1, -1))

    def return_fields(coefs):
        parts = lax.all_to_all(
            coefs.reshape(pw_count, message, 2 * harmonics), "pw", 0, 0, tiled=True
        )
        applied = pl.pallas_call(
            potential_kernel,
            in_specs=vmem(2),
            out_specs=vmem(1)[0],
            out_shape=shape((pw_count, message, 2 * harmonics), bf16),
            name="potential",
        )(parts, matrices)
        applied = lax.all_to_all(applied, "pw", 0, 0, tiled=True)
        own = pl.pallas_call(
            return_kernel,
            in_specs=vmem(5),
            out_specs=vmem(1)[0],
            out_shape=fields_shape,
            scratch_shapes=[pltpu.VMEM((CHUNK * rows, 4 * harmonics), bf16)],
            name="back",
        )(applied.reshape(atoms // 2 * rows, 2 * harmonics), template, cosine, sine, select)
        others = [
            lax.ppermute(own, "atom", [(source, source ^ flip) for source in range(group_count)])
            for flip in range(1, group_count)
        ]
        return [own] + others

    parts = return_fields(coefs)
    once, coefs = pl.pallas_call(
        next_kernel,
        in_specs=smem(1) + vmem(10),
        out_specs=tuple(vmem(2)),
        out_shape=(fields_shape, coefs_shape),
        scratch_shapes=[wave_scratch],
        name="next",
    )(reciprocal, fields, miller, *parts, template, cosine, sine, select)
    parts = return_fields(coefs)
    twice = pl.pallas_call(
        last_kernel,
        in_specs=smem(1) + vmem(6),
        out_specs=vmem(1)[0],
        out_shape=fields_shape,
        name="last",
    )(reciprocal, once, miller, *parts)
    return once.reshape(bands_in.shape), twice.reshape(bands_in.shape)


def solution(mesh):
    in_specs = (
        P(None, None, "pw"),
        P(None, None, "pw"),
        P(("pw", "atom"), None),
        P(None, "pw"),
        P(),
        P(),
        P(),
        P(),
    )
    out_specs = (P(None, None, "pw"), P(None, None, "pw"))
    return jax.shard_map(
        per_device, mesh=mesh, in_specs=in_specs, out_specs=out_specs, check_vma=False
    )
```

```python
import functools

import jax
import jax.numpy as jnp
from jax import lax
from jax.experimental import pallas as pl
from jax.experimental.pallas import tpu as pltpu
from jax.sharding import Mesh
from jax.sharding import PartitionSpec as P

f32 = jnp.float32
bf16 = jnp.bfloat16

COS_TURN = (
    0.9999999890590225,
    -19.739204499453912,
    64.93911745989556,
    -85.45013953088248,
    60.167630950949295,
    -25.96759924849463,
    6.528658161366808,
)
SIN_TURN = (
    6.283185302511503,
    -41.34170040531749,
    81.60513138579344,
    -76.70301535379849,
    42.02592698556796,
    -14.899846667364866,
    3.238137509743233,
)
NT = (((1,), (1,)), ((), ()))
NN = (((1,), (0,)), ((), ()))
CHUNK = 16


def dot(left, right, dims):
    return lax.dot_general(left, right, dims, preferred_element_type=f32)


def horner(coefs, arg):
    total = jnp.full_like(arg, coefs[-1])
    for coef in coefs[-2::-1]:
        total = total * arg + coef
    return total


def three_parts(values):
    high = values.astype(bf16)
    rest = values - high.astype(f32)
    middle = rest.astype(bf16)
    low = (rest - middle.astype(f32)).astype(bf16)
    return high, middle, low


def atom_table(positions, species, order, group, rows, groups, slot_dev):
    atoms = order.shape[1]
    row = lax.broadcasted_iota(jnp.int32, (rows, atoms), 0)
    lane = lax.broadcasted_iota(jnp.int32, (rows, atoms), 1)
    slot = (row // slot_dev * groups + group) * slot_dev + row % slot_dev
    pick_slot = jnp.where(lane == slot, 1.0, 0.0).astype(bf16)
    coarse, fine = order // 128, order % 128
    pad = jnp.zeros((14, atoms), f32)
    digits = jnp.concatenate([coarse.astype(f32), fine.astype(f32), pad], axis=0).astype(bf16)
    found = dot(pick_slot, digits, NT)
    atom = (found[:, 0:1] * 128.0 + found[:, 1:2]).astype(jnp.int32)
    pick_atom = jnp.where(lane == atom, 1.0, 0.0).astype(bf16)
    high, middle, low = three_parts(positions)
    pad = jnp.zeros((6, atoms), bf16)
    facts = jnp.concatenate([high, middle, low, species.astype(f32).astype(bf16), pad], axis=0)
    return dot(pick_atom, facts, NT)


def field_pair(fields):
    half = fields.shape[0] // 2
    return fields, jnp.concatenate([-fields[half:, :], fields[:half, :]], axis=0)


def project_weights(template):
    return jnp.concatenate([template, template[64:, :], template[:64, :]], axis=0)


def phases_of(table, miller):
    turns = jnp.zeros((table.shape[0], miller.shape[1]), f32)
    for axis in range(3):
        centre = table[:, axis : axis + 1] + table[:, 3 + axis : 4 + axis]
        centre = centre + table[:, 6 + axis : 7 + axis]
        turns = turns + centre * miller[axis : axis + 1, :]
    turns = turns - jnp.round(turns)
    square = turns * turns
    return horner(COS_TURN, square), turns * horner(SIN_TURN, square)


def prepare_kernel(
    groups, slot_dev, group_ref, miller_ref, positions_ref, species_ref, order_ref,
    cos_ref, sin_ref, select_ref, table_ref,
):
    atoms = cos_ref.shape[0]
    table_ref[...] = atom_table(
        positions_ref[...], species_ref[...], order_ref[...], group_ref[0], atoms, groups, slot_dev
    )
    miller = miller_ref[...].astype(f32)
    low = lax.broadcasted_iota(jnp.int32, (1, 128), 1) < 64

    def step(block, carry):
        base = pl.multiple_of(block * CHUNK, CHUNK)
        table = table_ref[pl.ds(base, CHUNK), :]
        cosine, sine = phases_of(table, miller)
        cos_ref[pl.ds(base, CHUNK), :] = cosine
        sin_ref[pl.ds(base, CHUNK), :] = sine
        kinds = table[:, 9:10]
        picked = []
        for pair in range(CHUNK // 2):
            even = 1.0 - kinds[2 * pair : 2 * pair + 1, :]
            odd = kinds[2 * pair + 1 : 2 * pair + 2, :]
            picked.append(jnp.where(low, even, odd))
        size = CHUNK // 2
        select_ref[pl.ds(pl.multiple_of(block * size, size), size), :] = jnp.concatenate(
            picked, axis=0
        )
        return carry

    lax.fori_loop(0, atoms // CHUNK, step, 0)


def project_chunk(base, phases, fields, weights, select, out_ref, wave_ref):
    rows = fields[0][0].shape[0]
    both = None
    for side in range(2):
        cosine, sine = phases[side]
        straight, turned = fields[side]
        for atom in range(CHUNK):
            wave = cosine[atom : atom + 1, :] * straight + sine[atom : atom + 1, :] * turned
            wave_ref[side, atom * rows : (atom + 1) * rows, :] = wave.astype(bf16)
        product = dot(wave_ref[side], weights[side], NT)
        both = product if both is None else both + product
    low = lax.broadcasted_iota(jnp.int32, (rows, 128), 1) < 64
    for pair in range(CHUNK // 2):
        even = both[2 * pair * rows : (2 * pair + 1) * rows, :]
        odd = both[(2 * pair + 1) * rows : (2 * pair + 2) * rows, :]
        first = jnp.where(low, even[:, :128], odd[:, :128])
        second = jnp.where(low, even[:, 128:], odd[:, 128:])
        mask = select[pair : pair + 1, :]
        chosen = first * mask + second * (1.0 - mask)
        start = pl.multiple_of((base // 2 + pair) * rows, rows)
        out_ref[pl.ds(start, rows), :] = chosen.astype(bf16)


def first_kernel(
    table_ref, miller_ref, own_fields_ref, fields_ref, own_template_ref, template_ref,
    own_cos_ref, own_sin_ref, select_ref, out_ref, cos_ref, sin_ref, wave_ref,
):
    miller = miller_ref[...].astype(f32)
    fields = [field_pair(own_fields_ref[...]), field_pair(fields_ref[...])]
    weights = [project_weights(own_template_ref[...]), project_weights(template_ref[...])]

    def step(block, carry):
        base = pl.multiple_of(block * CHUNK, CHUNK)
        chunk = pl.ds(base, CHUNK)
        other = phases_of(table_ref[chunk, :], miller)
        cos_ref[chunk, :] = other[0]
        sin_ref[chunk, :] = other[1]
        phases = [(own_cos_ref[chunk, :], own_sin_ref[chunk, :]), other]
        size = CHUNK // 2
        select = select_ref[pl.ds(pl.multiple_of(block * size, size), size), :]
        project_chunk(base, phases, fields, weights, select, out_ref, wave_ref)
        return carry

    lax.fori_loop(0, cos_ref.shape[0] // CHUNK, step, 0)


def kinetic_of(miller_ref, lengths_ref):
    miller = miller_ref[...].astype(f32)
    total = jnp.zeros((1, miller.shape[1]), f32)
    for axis in range(3):
        wave_number = lengths_ref[axis] * miller[axis : axis + 1, :]
        total = total + wave_number * wave_number
    return 0.5 * total


def next_kernel(
    lengths_ref, own_miller_ref, miller_ref, own_fields_ref, fields_ref, mine_ref, low_ref,
    high_ref, both_ref, own_template_ref, template_ref, own_cos_ref, own_sin_ref, cos_ref, sin_ref,
    select_ref, fields_out_ref, out_ref, wave_ref,
):
    own = kinetic_of(own_miller_ref, lengths_ref) * own_fields_ref[...]
    own = own + ((mine_ref[0] + high_ref[0]) + (low_ref[1] + both_ref[1]))
    fields_out_ref[...] = own
    other = kinetic_of(miller_ref, lengths_ref) * fields_ref[...]
    other = other + ((mine_ref[1] + high_ref[1]) + (low_ref[0] + both_ref[0]))
    fields = [field_pair(own), field_pair(other)]
    weights = [project_weights(own_template_ref[...]), project_weights(template_ref[...])]

    def step(block, carry):
        base = pl.multiple_of(block * CHUNK, CHUNK)
        chunk = pl.ds(base, CHUNK)
        phases = [
            (own_cos_ref[chunk, :], own_sin_ref[chunk, :]),
            (cos_ref[chunk, :], sin_ref[chunk, :]),
        ]
        size = CHUNK // 2
        select = select_ref[pl.ds(pl.multiple_of(block * size, size), size), :]
        project_chunk(base, phases, fields, weights, select, out_ref, wave_ref)
        return carry

    lax.fori_loop(0, cos_ref.shape[0] // CHUNK, step, 0)


def last_kernel(
    lengths_ref, miller_ref, fields_ref, mine_ref, low_ref, high_ref, both_ref, fields_out_ref
):
    total = kinetic_of(miller_ref, lengths_ref) * fields_ref[...]
    fields_out_ref[...] = total + ((mine_ref[0] + high_ref[...]) + (low_ref[...] + both_ref[...]))


def potential_kernel(parts_ref, potential_ref, out_ref):
    summed = jnp.sum(parts_ref[...].astype(f32), axis=0)
    pairs = potential_ref.shape[0]
    rows = summed.shape[0] // pairs
    half = rows // 2
    low = lax.broadcasted_iota(jnp.int32, (64, 128), 1) < 64
    results = []
    for pair in range(pairs):
        blocks = []
        for part in range(2):
            matrices = potential_ref[pair, part].astype(f32)
            blocks.append(jnp.where(low, matrices, 0.0))
            blocks.append(jnp.where(low, 0.0, matrices))
        weights = jnp.concatenate(blocks, axis=0).astype(bf16)
        pieces = jnp.concatenate(three_parts(summed[pair * rows : (pair + 1) * rows, :]), axis=0)
        product = dot(pieces, weights, NT)
        product = product[2 * rows :, :] + product[rows : 2 * rows, :] + product[:rows, :]
        real, imag = product[:, :128], product[:, 128:]
        results.append(real[:half, :] - imag[half:, :])
        results.append(real[half:, :] + imag[:half, :])
    applied = jnp.concatenate(results, axis=0).astype(bf16)
    out_ref[...] = jnp.broadcast_to(applied[None], out_ref.shape)


def return_kernel(
    applied_ref, own_template_ref, template_ref, own_cos_ref, own_sin_ref, cos_ref, sin_ref,
    select_ref, out_ref, stack_ref,
):
    atoms = cos_ref.shape[0]
    _, rows, waves = out_ref.shape
    half = rows // 2
    weights = []
    for ref in (own_template_ref, template_ref):
        low, high = ref[:64, :], ref[64:, :]
        weights.append(jnp.concatenate([low, low, high, high], axis=0))
    low = jnp.where(lax.broadcasted_iota(jnp.int32, (1, 128), 1) < 64, 1.0, 0.0)
    zero = jnp.zeros((rows, waves), f32)

    def step(block, carry):
        base = pl.multiple_of(block * CHUNK, CHUNK)
        chunk = pl.ds(base, CHUNK)
        size = CHUNK // 2
        select = select_ref[pl.ds(pl.multiple_of(block * size, size), size), :]
        for pair in range(CHUNK // 2):
            start = pl.multiple_of((base // 2 + pair) * rows, rows)
            applied = applied_ref[pl.ds(start, rows), :].astype(f32)
            mask = select[pair : pair + 1, :]
            is_first = low * mask + (1.0 - low) * (1.0 - mask)
            kept, other = applied * is_first, applied * (1.0 - is_first)
            top = slice(2 * pair * rows, (2 * pair + 1) * rows)
            bottom = slice((2 * pair + 1) * rows, (2 * pair + 2) * rows)
            stack_ref[top, :128] = (kept * low).astype(bf16)
            stack_ref[top, 128:] = (other * low).astype(bf16)
            stack_ref[bottom, :128] = (kept * (1.0 - low)).astype(bf16)
            stack_ref[bottom, 128:] = (other * (1.0 - low)).astype(bf16)
        sums = []
        for side, (cosines, sines) in enumerate(((own_cos_ref, own_sin_ref), (cos_ref, sin_ref))):
            straight, turned = carry[side]
            cosine, sine = cosines[chunk, :], sines[chunk, :]
            images = dot(stack_ref[...], weights[side], NN)
            for atom in range(CHUNK):
                image = images[atom * rows : (atom + 1) * rows, :]
                straight = straight + cosine[atom : atom + 1, :] * image
                turned = turned + sine[atom : atom + 1, :] * image
            sums.append((straight, turned))
        return tuple(sums)

    sums = lax.fori_loop(0, atoms // CHUNK, step, ((zero, zero), (zero, zero)))
    for side, (straight, turned) in enumerate(sums):
        out_ref[side, :half, :] = straight[:half, :] + turned[half:, :]
        out_ref[side, half:, :] = straight[half:, :] - turned[:half, :]


def vmem(count):
    return [pl.BlockSpec(memory_space=pltpu.VMEM)] * count


def smem(count):
    return [pl.BlockSpec(memory_space=pltpu.SMEM)] * count


def shape(dims, dtype):
    return jax.ShapeDtypeStruct(dims, dtype)


def flip(array, *axes):
    pairs = [(place, 2 ** len(axes) - 1 - place) for place in range(2 ** len(axes))]
    return lax.ppermute(array, axes, pairs)


def per_device(bands_in, template, potential, miller, positions, species, atom_order, reciprocal):
    plane = lax.axis_size("zx")
    groups = lax.axis_size("yh") * lax.axis_size("core")
    slot_dev = potential.shape[0]
    atoms = slot_dev * plane
    species_count, harmonics, waves = template.shape
    rows = 2 * bands_in.shape[1]
    pairs = slot_dev // 2
    message = pairs * rows
    width = 2 * harmonics
    template = template.reshape(species_count * harmonics, waves)
    fields = bands_in.reshape(rows, waves)
    matrices = potential.reshape(pairs, 2, 2, harmonics, harmonics)
    matrices = matrices.transpose(0, 2, 3, 1, 4).reshape(pairs, 2, harmonics, width)
    group = (lax.axis_index("yl") * plane * groups + lax.axis_index(("yh", "core"))).reshape(1)
    coefs_shape = shape((atoms // 2 * rows, width), bf16)
    fields_shape = shape((rows, waves), f32)
    phase_shape = shape((atoms, waves), f32)
    wave_scratch = pltpu.VMEM((2, CHUNK * rows, waves), bf16)

    other_miller = flip(miller, "yl")
    other_fields = flip(fields, "yl")
    other_template = flip(template, "yl")
    own_cos, own_sin, select, table = pl.pallas_call(
        functools.partial(prepare_kernel, groups, slot_dev),
        in_specs=smem(1) + vmem(4),
        out_specs=tuple(vmem(4)),
        out_shape=(
            phase_shape, phase_shape, shape((atoms // 2, 128), f32), shape((atoms, 16), f32)
        ),
        name="prepare",
    )(
        group.astype(jnp.int32), miller, positions, species.reshape(1, -1),
        atom_order.reshape(1, -1),
    )
    coefs, other_cos, other_sin = pl.pallas_call(
        first_kernel,
        in_specs=vmem(9),
        out_specs=tuple(vmem(3)),
        out_shape=(coefs_shape, phase_shape, phase_shape),
        scratch_shapes=[wave_scratch],
        name="first",
    )(
        table, other_miller, fields, other_fields, template, other_template, own_cos, own_sin,
        select,
    )
    fixed = (template, other_template, own_cos, own_sin, other_cos, other_sin, select)

    def return_fields(coefs):
        parts = lax.all_to_all(coefs.reshape(plane, message, width), "zx", 0, 0, tiled=True)
        applied = pl.pallas_call(
            potential_kernel,
            in_specs=vmem(2),
            out_specs=vmem(1)[0],
            out_shape=shape((plane, message, width), bf16),
            name="potential",
        )(parts, matrices)
        applied = lax.all_to_all(applied, "zx", 0, 0, tiled=True)
        own = pl.pallas_call(
            return_kernel,
            in_specs=vmem(8),
            out_specs=vmem(1)[0],
            out_shape=shape((2, rows, waves), f32),
            scratch_shapes=[pltpu.VMEM((CHUNK * rows, 2 * width), bf16)],
            name="back",
        )(applied.reshape(atoms // 2 * rows, width), *fixed)
        return own + flip(own, "core")

    mine = return_fields(coefs)
    once, coefs = pl.pallas_call(
        next_kernel,
        in_specs=smem(1) + vmem(15),
        out_specs=tuple(vmem(2)),
        out_shape=(fields_shape, coefs_shape),
        scratch_shapes=[wave_scratch],
        name="next",
    )(
        reciprocal, miller, other_miller, fields, other_fields, mine, flip(mine, "yl"),
        flip(mine, "yh"), flip(mine, "yl", "yh"), *fixed,
    )
    mine = return_fields(coefs)
    twice = pl.pallas_call(
        last_kernel,
        in_specs=smem(1) + vmem(6),
        out_specs=vmem(1)[0],
        out_shape=fields_shape,
        name="last",
    )(
        reciprocal, miller, once, mine, flip(mine[1], "yl"), flip(mine[0], "yh"),
        flip(mine[1], "yl", "yh"),
    )
    return once.reshape(bands_in.shape), twice.reshape(bands_in.shape)


def solution(mesh):
    pw, groups = mesh.devices.shape
    fine = Mesh(mesh.devices.reshape(2, pw // 2, 2, groups // 2), ("yl", "zx", "yh", "core"))
    waves, slots = ("yl", "zx"), ("yl", "zx", "yh", "core")
    in_specs = (
        P(None, None, waves),
        P(None, None, waves),
        P(slots, None),
        P(None, waves),
        P(),
        P(),
        P(),
        P(),
    )
    out_specs = (P(None, None, waves), P(None, None, waves))
    return jax.shard_map(
        per_device, mesh=fine, in_specs=in_specs, out_specs=out_specs, check_vma=False
    )
```

```python
import functools

import jax
import jax.numpy as jnp
from jax import lax
from jax.experimental import pallas as pl
from jax.experimental.pallas import tpu as pltpu
from jax.sharding import Mesh
from jax.sharding import PartitionSpec as P

f32 = jnp.float32
bf16 = jnp.bfloat16

COS_TURN = (
    0.9999999890590225,
    -19.739204499453912,
    64.93911745989556,
    -85.45013953088248,
    60.167630950949295,
    -25.96759924849463,
    6.528658161366808,
)
SIN_TURN = (
    6.283185302511503,
    -41.34170040531749,
    81.60513138579344,
    -76.70301535379849,
    42.02592698556796,
    -14.899846667364866,
    3.238137509743233,
)
NT = (((1,), (1,)), ((), ()))
NN = (((1,), (0,)), ((), ()))
CHUNK = 16
LIMIT = pltpu.CompilerParams(vmem_limit_bytes=12 * 2**20)


def dot(left, right, dims):
    return lax.dot_general(left, right, dims, preferred_element_type=f32)


def horner(coefs, arg):
    total = jnp.full_like(arg, coefs[-1])
    for coef in coefs[-2::-1]:
        total = total * arg + coef
    return total


def three_parts(values):
    high = values.astype(bf16)
    rest = values - high.astype(f32)
    middle = rest.astype(bf16)
    low = (rest - middle.astype(f32)).astype(bf16)
    return high, middle, low


def atom_table(positions, species, order, group, rows, groups, slot_dev):
    atoms = order.shape[1]
    row = lax.broadcasted_iota(jnp.int32, (rows, atoms), 0)
    lane = lax.broadcasted_iota(jnp.int32, (rows, atoms), 1)
    slot = (row // slot_dev * groups + group) * slot_dev + row % slot_dev
    pick_slot = jnp.where(lane == slot, 1.0, 0.0).astype(bf16)
    coarse, fine = order // 128, order % 128
    pad = jnp.zeros((14, atoms), f32)
    digits = jnp.concatenate([coarse.astype(f32), fine.astype(f32), pad], axis=0).astype(bf16)
    found = dot(pick_slot, digits, NT)
    atom = (found[:, 0:1] * 128.0 + found[:, 1:2]).astype(jnp.int32)
    pick_atom = jnp.where(lane == atom, 1.0, 0.0).astype(bf16)
    high, middle, low = three_parts(positions)
    pad = jnp.zeros((6, atoms), bf16)
    facts = jnp.concatenate([high, middle, low, species.astype(f32).astype(bf16), pad], axis=0)
    return dot(pick_atom, facts, NT)


def field_pair(fields):
    half = fields.shape[0] // 2
    return fields, jnp.concatenate([-fields[half:, :], fields[:half, :]], axis=0)


def project_weights(template):
    return jnp.concatenate([template, template[64:, :], template[:64, :]], axis=0)


def phases_of(table, miller):
    turns = jnp.zeros((table.shape[0], miller.shape[1]), f32)
    for axis in range(3):
        centre = table[:, axis : axis + 1] + table[:, 3 + axis : 4 + axis]
        centre = centre + table[:, 6 + axis : 7 + axis]
        turns = turns + centre * miller[axis : axis + 1, :]
    turns = turns - jnp.round(turns)
    square = turns * turns
    return horner(COS_TURN, square), turns * horner(SIN_TURN, square)


def prepare_kernel(
    groups, slot_dev, group_ref, miller_ref, positions_ref, species_ref, order_ref,
    cos_ref, sin_ref, select_ref, table_ref,
):
    atoms = cos_ref.shape[0]
    table_ref[...] = atom_table(
        positions_ref[...], species_ref[...], order_ref[...], group_ref[0], atoms, groups, slot_dev
    )
    miller = miller_ref[...].astype(f32)
    low = lax.broadcasted_iota(jnp.int32, (1, 128), 1) < 64

    def step(block, carry):
        base = pl.multiple_of(block * CHUNK, CHUNK)
        table = table_ref[pl.ds(base, CHUNK), :]
        cosine, sine = phases_of(table, miller)
        cos_ref[pl.ds(base, CHUNK), :] = cosine
        sin_ref[pl.ds(base, CHUNK), :] = sine
        kinds = table[:, 9:10]
        picked = []
        for pair in range(CHUNK // 2):
            even = 1.0 - kinds[2 * pair : 2 * pair + 1, :]
            odd = kinds[2 * pair + 1 : 2 * pair + 2, :]
            picked.append(jnp.where(low, even, odd))
        size = CHUNK // 2
        select_ref[pl.ds(pl.multiple_of(block * size, size), size), :] = jnp.concatenate(
            picked, axis=0
        )
        return carry

    lax.fori_loop(0, atoms // CHUNK, step, 0)


def project_chunk(base, phases, fields, weights, select, out_ref, wave_ref):
    rows = fields[0][0].shape[0]
    both = None
    for side in range(2):
        cosine, sine = phases[side]
        straight, turned = fields[side]
        for atom in range(CHUNK):
            wave = cosine[atom : atom + 1, :] * straight + sine[atom : atom + 1, :] * turned
            wave_ref[side, atom * rows : (atom + 1) * rows, :] = wave.astype(bf16)
        product = dot(wave_ref[side], weights[side], NT)
        both = product if both is None else both + product
    low = lax.broadcasted_iota(jnp.int32, (rows, 128), 1) < 64
    for pair in range(CHUNK // 2):
        even = both[2 * pair * rows : (2 * pair + 1) * rows, :]
        odd = both[(2 * pair + 1) * rows : (2 * pair + 2) * rows, :]
        first = jnp.where(low, even[:, :128], odd[:, :128])
        second = jnp.where(low, even[:, 128:], odd[:, 128:])
        mask = select[pair : pair + 1, :]
        chosen = first * mask + second * (1.0 - mask)
        start = pl.multiple_of((base // 2 + pair) * rows, rows)
        out_ref[pl.ds(start, rows), :] = chosen.astype(bf16)


def first_kernel(
    table_ref, miller_ref, own_fields_ref, fields_ref, own_template_ref, template_ref,
    own_cos_ref, own_sin_ref, select_ref, out_ref, cos_ref, sin_ref, wave_ref,
):
    miller = miller_ref[...].astype(f32)
    fields = [field_pair(own_fields_ref[...]), field_pair(fields_ref[...])]
    weights = [project_weights(own_template_ref[...]), project_weights(template_ref[...])]

    def step(block, carry):
        base = pl.multiple_of(block * CHUNK, CHUNK)
        chunk = pl.ds(base, CHUNK)
        other = phases_of(table_ref[chunk, :], miller)
        cos_ref[chunk, :] = other[0]
        sin_ref[chunk, :] = other[1]
        phases = [(own_cos_ref[chunk, :], own_sin_ref[chunk, :]), other]
        size = CHUNK // 2
        select = select_ref[pl.ds(pl.multiple_of(block * size, size), size), :]
        project_chunk(base, phases, fields, weights, select, out_ref, wave_ref)
        return carry

    lax.fori_loop(0, cos_ref.shape[0] // CHUNK, step, 0)


def kinetic_of(miller_ref, lengths_ref):
    miller = miller_ref[...].astype(f32)
    total = jnp.zeros((1, miller.shape[1]), f32)
    for axis in range(3):
        wave_number = lengths_ref[axis] * miller[axis : axis + 1, :]
        total = total + wave_number * wave_number
    return 0.5 * total


def next_kernel(
    lengths_ref, own_miller_ref, miller_ref, own_fields_ref, fields_ref, mine_ref, low_ref,
    high_ref, both_ref, own_template_ref, template_ref, own_cos_ref, own_sin_ref, cos_ref, sin_ref,
    select_ref, fields_out_ref, out_ref, wave_ref,
):
    own = kinetic_of(own_miller_ref, lengths_ref) * own_fields_ref[...]
    own = own + ((mine_ref[0] + high_ref[0]) + (low_ref[1] + both_ref[1]))
    fields_out_ref[...] = own
    other = kinetic_of(miller_ref, lengths_ref) * fields_ref[...]
    other = other + ((mine_ref[1] + high_ref[1]) + (low_ref[0] + both_ref[0]))
    fields = [field_pair(own), field_pair(other)]
    weights = [project_weights(own_template_ref[...]), project_weights(template_ref[...])]

    def step(block, carry):
        base = pl.multiple_of(block * CHUNK, CHUNK)
        chunk = pl.ds(base, CHUNK)
        phases = [
            (own_cos_ref[chunk, :], own_sin_ref[chunk, :]),
            (cos_ref[chunk, :], sin_ref[chunk, :]),
        ]
        size = CHUNK // 2
        select = select_ref[pl.ds(pl.multiple_of(block * size, size), size), :]
        project_chunk(base, phases, fields, weights, select, out_ref, wave_ref)
        return carry

    lax.fori_loop(0, cos_ref.shape[0] // CHUNK, step, 0)


def last_kernel(
    lengths_ref, miller_ref, fields_ref, mine_ref, low_ref, high_ref, both_ref, fields_out_ref
):
    total = kinetic_of(miller_ref, lengths_ref) * fields_ref[...]
    fields_out_ref[...] = total + ((mine_ref[0] + high_ref[...]) + (low_ref[...] + both_ref[...]))


def potential_kernel(parts_ref, potential_ref, out_ref):
    summed = jnp.sum(parts_ref[...].astype(f32), axis=0)
    pairs = potential_ref.shape[0]
    rows = summed.shape[0] // pairs
    half = rows // 2
    low = lax.broadcasted_iota(jnp.int32, (64, 128), 1) < 64
    results = []
    for pair in range(pairs):
        blocks = []
        for part in range(2):
            matrices = potential_ref[pair, part].astype(f32)
            blocks.append(jnp.where(low, matrices, 0.0))
            blocks.append(jnp.where(low, 0.0, matrices))
        weights = jnp.concatenate(blocks, axis=0).astype(bf16)
        pieces = jnp.concatenate(three_parts(summed[pair * rows : (pair + 1) * rows, :]), axis=0)
        product = dot(pieces, weights, NT)
        product = product[2 * rows :, :] + product[rows : 2 * rows, :] + product[:rows, :]
        real, imag = product[:, :128], product[:, 128:]
        results.append(real[:half, :] - imag[half:, :])
        results.append(real[half:, :] + imag[:half, :])
    applied = jnp.concatenate(results, axis=0).astype(bf16)
    out_ref[...] = jnp.broadcast_to(applied[None], out_ref.shape)


def return_kernel(
    applied_ref, own_template_ref, template_ref, own_cos_ref, own_sin_ref, cos_ref, sin_ref,
    select_ref, out_ref, stack_ref,
):
    atoms = cos_ref.shape[0]
    _, rows, waves = out_ref.shape
    half = rows // 2
    weights = []
    for ref in (own_template_ref, template_ref):
        low, high = ref[:64, :], ref[64:, :]
        weights.append(jnp.concatenate([low, low, high, high], axis=0))
    low = jnp.where(lax.broadcasted_iota(jnp.int32, (1, 128), 1) < 64, 1.0, 0.0)
    zero = jnp.zeros((rows, waves), f32)

    def step(block, carry):
        base = pl.multiple_of(block * CHUNK, CHUNK)
        chunk = pl.ds(base, CHUNK)
        size = CHUNK // 2
        select = select_ref[pl.ds(pl.multiple_of(block * size, size), size), :]
        for pair in range(CHUNK // 2):
            start = pl.multiple_of((base // 2 + pair) * rows, rows)
            applied = applied_ref[pl.ds(start, rows), :].astype(f32)
            mask = select[pair : pair + 1, :]
            is_first = low * mask + (1.0 - low) * (1.0 - mask)
            kept, other = applied * is_first, applied * (1.0 - is_first)
            top = slice(2 * pair * rows, (2 * pair + 1) * rows)
            bottom = slice((2 * pair + 1) * rows, (2 * pair + 2) * rows)
            stack_ref[top, :128] = (kept * low).astype(bf16)
            stack_ref[top, 128:] = (other * low).astype(bf16)
            stack_ref[bottom, :128] = (kept * (1.0 - low)).astype(bf16)
            stack_ref[bottom, 128:] = (other * (1.0 - low)).astype(bf16)
        sums = []
        for side, (cosines, sines) in enumerate(((own_cos_ref, own_sin_ref), (cos_ref, sin_ref))):
            straight, turned = carry[side]
            cosine, sine = cosines[chunk, :], sines[chunk, :]
            images = dot(stack_ref[...], weights[side], NN)
            for atom in range(CHUNK):
                image = images[atom * rows : (atom + 1) * rows, :]
                straight = straight + cosine[atom : atom + 1, :] * image
                turned = turned + sine[atom : atom + 1, :] * image
            sums.append((straight, turned))
        return tuple(sums)

    sums = lax.fori_loop(0, atoms // CHUNK, step, ((zero, zero), (zero, zero)))
    for side, (straight, turned) in enumerate(sums):
        out_ref[side, :half, :] = straight[:half, :] + turned[half:, :]
        out_ref[side, half:, :] = straight[half:, :] - turned[:half, :]


def vmem(count):
    return [pl.BlockSpec(memory_space=pltpu.VMEM)] * count


def smem(count):
    return [pl.BlockSpec(memory_space=pltpu.SMEM)] * count


def shape(dims, dtype):
    return jax.ShapeDtypeStruct(dims, dtype)


def flip(array, *axes):
    pairs = [(place, 2 ** len(axes) - 1 - place) for place in range(2 ** len(axes))]
    return lax.ppermute(array, axes, pairs)


def per_device(bands_in, template, potential, miller, positions, species, atom_order, reciprocal):
    plane = lax.axis_size("zx")
    groups = lax.axis_size("yh") * lax.axis_size("core")
    slot_dev = potential.shape[0]
    atoms = slot_dev * plane
    species_count, harmonics, waves = template.shape
    rows = 2 * bands_in.shape[1]
    pairs = slot_dev // 2
    message = pairs * rows
    width = 2 * harmonics
    template = template.reshape(species_count * harmonics, waves)
    fields = bands_in.reshape(rows, waves)
    matrices = potential.reshape(pairs, 2, 2, harmonics, harmonics)
    matrices = matrices.transpose(0, 2, 3, 1, 4).reshape(pairs, 2, harmonics, width)
    group = (lax.axis_index("yl") * plane * groups + lax.axis_index(("yh", "core"))).reshape(1)
    coefs_shape = shape((atoms // 2 * rows, width), bf16)
    fields_shape = shape((rows, waves), f32)
    phase_shape = shape((atoms, waves), f32)
    wave_scratch = pltpu.VMEM((2, CHUNK * rows, waves), bf16)

    other_miller = flip(miller, "yl")
    other_fields = flip(fields, "yl")
    other_template = flip(template, "yl")
    own_cos, own_sin, select, table = pl.pallas_call(
        functools.partial(prepare_kernel, groups, slot_dev),
        in_specs=smem(1) + vmem(4),
        out_specs=tuple(vmem(4)),
        out_shape=(
            phase_shape, phase_shape, shape((atoms // 2, 128), f32), shape((atoms, 16), f32)
        ),
        compiler_params=LIMIT,
        name="prepare",
    )(
        group.astype(jnp.int32), miller, positions, species.reshape(1, -1),
        atom_order.reshape(1, -1),
    )
    coefs, other_cos, other_sin = pl.pallas_call(
        first_kernel,
        in_specs=vmem(9),
        out_specs=tuple(vmem(3)),
        out_shape=(coefs_shape, phase_shape, phase_shape),
        scratch_shapes=[wave_scratch],
        compiler_params=LIMIT,
        name="first",
    )(
        table, other_miller, fields, other_fields, template, other_template, own_cos, own_sin,
        select,
    )
    fixed = (template, other_template, own_cos, own_sin, other_cos, other_sin, select)

    def return_fields(coefs):
        parts = lax.all_to_all(coefs.reshape(plane, message, width), "zx", 0, 0, tiled=True)
        applied = pl.pallas_call(
            potential_kernel,
            in_specs=vmem(2),
            out_specs=vmem(1)[0],
            out_shape=shape((plane, message, width), bf16),
            compiler_params=LIMIT,
        name="potential",
        )(parts, matrices)
        applied = lax.all_to_all(applied, "zx", 0, 0, tiled=True)
        own = pl.pallas_call(
            return_kernel,
            in_specs=vmem(8),
            out_specs=vmem(1)[0],
            out_shape=shape((2, rows, waves), f32),
            scratch_shapes=[pltpu.VMEM((CHUNK * rows, 2 * width), bf16)],
            compiler_params=LIMIT,
        name="back",
        )(applied.reshape(atoms // 2 * rows, width), *fixed)
        return own + flip(own, "core")

    mine = return_fields(coefs)
    once, coefs = pl.pallas_call(
        next_kernel,
        in_specs=smem(1) + vmem(15),
        out_specs=tuple(vmem(2)),
        out_shape=(fields_shape, coefs_shape),
        scratch_shapes=[wave_scratch],
        compiler_params=LIMIT,
        name="next",
    )(
        reciprocal, miller, other_miller, fields, other_fields, mine, flip(mine, "yl"),
        flip(mine, "yh"), flip(mine, "yl", "yh"), *fixed,
    )
    mine = return_fields(coefs)
    twice = pl.pallas_call(
        last_kernel,
        in_specs=smem(1) + vmem(6),
        out_specs=vmem(1)[0],
        out_shape=fields_shape,
        compiler_params=LIMIT,
        name="last",
    )(
        reciprocal, miller, once, mine, flip(mine[1], "yl"), flip(mine[0], "yh"),
        flip(mine[1], "yl", "yh"),
    )
    return once.reshape(bands_in.shape), twice.reshape(bands_in.shape)


def solution(mesh):
    pw, groups = mesh.devices.shape
    fine = Mesh(mesh.devices.reshape(2, pw // 2, 2, groups // 2), ("yl", "zx", "yh", "core"))
    waves, slots = ("yl", "zx"), ("yl", "zx", "yh", "core")
    in_specs = (
        P(None, None, waves),
        P(None, None, waves),
        P(slots, None),
        P(None, waves),
        P(),
        P(),
        P(),
        P(),
    )
    out_specs = (P(None, None, waves), P(None, None, waves))
    return jax.shard_map(
        per_device, mesh=fine, in_specs=in_specs, out_specs=out_specs, check_vma=False
    )
```

```python
import functools

import jax
import jax.numpy as jnp
from jax import lax
from jax.experimental import pallas as pl
from jax.experimental.pallas import tpu as pltpu
from jax.sharding import Mesh
from jax.sharding import PartitionSpec as P

f32 = jnp.float32
bf16 = jnp.bfloat16

COS_TURN = (
    0.9999999890590225,
    -19.739204499453912,
    64.93911745989556,
    -85.45013953088248,
    60.167630950949295,
    -25.96759924849463,
    6.528658161366808,
)
SIN_TURN = (
    6.283185302511503,
    -41.34170040531749,
    81.60513138579344,
    -76.70301535379849,
    42.02592698556796,
    -14.899846667364866,
    3.238137509743233,
)
NT = (((1,), (1,)), ((), ()))
NN = (((1,), (0,)), ((), ()))
CHUNK = 128
STEP = 128
LIMIT = pltpu.CompilerParams(vmem_limit_bytes=12 * 2**20)


def dot(left, right, dims):
    return lax.dot_general(left, right, dims, preferred_element_type=f32)


def horner(coefs, arg):
    total = jnp.full_like(arg, coefs[-1])
    for coef in coefs[-2::-1]:
        total = total * arg + coef
    return total


def three_parts(values):
    high = values.astype(bf16)
    rest = values - high.astype(f32)
    middle = rest.astype(bf16)
    low = (rest - middle.astype(f32)).astype(bf16)
    return high, middle, low


def atom_table(positions, species, order, first_slot, core, rows, stride, slot_dev):
    atoms = order.shape[1]
    row = lax.broadcasted_iota(jnp.int32, (rows, 1), 0)
    pair = 2 * slot_dev
    side = (row % pair // slot_dev) ^ core
    slot = first_slot + row // pair * stride + side * slot_dev + row % slot_dev
    lane = lax.broadcasted_iota(jnp.int32, (rows, atoms), 1)
    pick_slot = jnp.where(lane == slot, 1.0, 0.0).astype(bf16)
    coarse, fine = order // 128, order % 128
    pad = jnp.zeros((14, atoms), f32)
    digits = jnp.concatenate([coarse.astype(f32), fine.astype(f32), pad], axis=0).astype(bf16)
    found = dot(pick_slot, digits, NT)
    atom = (found[:, 0:1] * 128.0 + found[:, 1:2]).astype(jnp.int32)
    pick_atom = jnp.where(lane == atom, 1.0, 0.0).astype(bf16)
    high, middle, low = three_parts(positions)
    pad = jnp.zeros((6, atoms), bf16)
    facts = jnp.concatenate([high, middle, low, species.astype(f32).astype(bf16), pad], axis=0)
    return dot(pick_atom, facts, NT)


def field_pair(fields):
    half = fields.shape[0] // 2
    return fields, jnp.concatenate([-fields[half:, :], fields[:half, :]], axis=0)


def core_bands(fields_ref, core):
    quarter = fields_ref.shape[0] // 4
    parts = [fields_ref[part * quarter : (part + 1) * quarter, :] for part in range(4)]
    first = jnp.concatenate([parts[0], parts[2]], axis=0)
    second = jnp.concatenate([parts[1], parts[3]], axis=0)
    return jnp.where(core == 0, first, second)


def phases_of(table, miller):
    turns = jnp.zeros((table.shape[0], miller.shape[1]), f32)
    for axis in range(3):
        centre = table[:, axis : axis + 1] + table[:, 3 + axis : 4 + axis]
        centre = centre + table[:, 6 + axis : 7 + axis]
        turns = turns + centre * miller[axis : axis + 1, :]
    turns = turns - jnp.round(turns)
    square = turns * turns
    return horner(COS_TURN, square), turns * horner(SIN_TURN, square)


def kinetic_of(miller, lengths):
    total = jnp.zeros((1, miller.shape[1]), f32)
    for axis in range(3):
        wave_number = lengths[:, axis : axis + 1] * miller[axis : axis + 1, :]
        total = total + wave_number * wave_number
    return 0.5 * total


def both_weights(template):
    low, high = template[:64, :], template[64:, :]
    return jnp.concatenate([low, high, high, low], axis=0)


def double_weights(template):
    low, high = template[:64, :], template[64:, :]
    return jnp.concatenate([low, low, high, high], axis=0)


def prepare_kernel(
    stride, slot_dev, place_ref, lengths_ref, miller_ref, positions_ref, species_ref, order_ref,
    fields_ref, template_ref, cos_ref, sin_ref, select_ref, table_ref, own_ref, kinetic_ref,
    both_ref, double_ref,
):
    atoms = cos_ref.shape[0]
    core = place_ref[:, 1:2]
    table_ref[...] = atom_table(
        positions_ref[...], species_ref[...], order_ref[...], place_ref[:, 0:1], core, atoms,
        stride, slot_dev,
    )
    miller = miller_ref[...].astype(f32)
    kinetic_ref[...] = kinetic_of(miller, lengths_ref[...])
    own_ref[...] = core_bands(fields_ref, core)
    both_ref[...] = both_weights(template_ref[...])
    double_ref[...] = double_weights(template_ref[...])
    low = lax.broadcasted_iota(jnp.int32, (1, 128), 1) < 64

    def step(block, carry):
        base = pl.multiple_of(block * STEP, STEP)
        table = table_ref[pl.ds(base, STEP), :]
        cosine, sine = phases_of(table, miller)
        cos_ref[pl.ds(base, STEP), :] = cosine
        sin_ref[pl.ds(base, STEP), :] = sine
        kinds = table[:, 9:10]
        picked = []
        for pair in range(STEP // 2):
            even = 1.0 - kinds[2 * pair : 2 * pair + 1, :]
            odd = kinds[2 * pair + 1 : 2 * pair + 2, :]
            picked.append(jnp.where(low, even, odd))
        half = pl.ds(pl.multiple_of(block * (STEP // 2), STEP // 2), STEP // 2)
        select_ref[half, :] = jnp.concatenate(picked, axis=0)
        return carry

    lax.fori_loop(0, atoms // STEP, step, 0)


def project_chunk(base, phases, fields, weights, select, out_ref, wave_ref):
    rows = fields[0][0].shape[0]
    products = []
    for side in range(2):
        cosine, sine = phases[side]
        straight, turned = fields[side]
        for pair in range(CHUNK // 2):
            waves = [
                cosine[atom : atom + 1, :] * straight + sine[atom : atom + 1, :] * turned
                for atom in (2 * pair, 2 * pair + 1)
            ]
            two = slice(2 * pair * rows, 2 * (pair + 1) * rows)
            wave_ref[side, two, :] = jnp.concatenate(waves, axis=0).astype(bf16)
        products.append(dot(wave_ref[side], weights[side][...], NT))
    both = products[0] + products[1]
    low = lax.broadcasted_iota(jnp.int32, (rows, 128), 1) < 64
    results = []
    for pair in range(CHUNK // 2):
        even = both[2 * pair * rows : (2 * pair + 1) * rows, :]
        odd = both[(2 * pair + 1) * rows : (2 * pair + 2) * rows, :]
        first = jnp.where(low, even[:, :128], odd[:, :128])
        second = jnp.where(low, even[:, 128:], odd[:, 128:])
        results.append(jnp.where(select[pair : pair + 1, :] > 0.5, first, second))
    size = CHUNK // 2 * rows
    start = pl.multiple_of(base // 2 * rows, size)
    out_ref[pl.ds(start, size), :] = jnp.concatenate(results, axis=0).astype(bf16)


def first_kernel(
    place_ref, lengths_ref, table_ref, miller_ref, own_ref, fields_ref, own_both_ref,
    template_ref, own_cos_ref, own_sin_ref, select_ref, out_ref, cos_ref, sin_ref, other_ref,
    kinetic_ref, both_ref, double_ref, wave_ref,
):
    miller = miller_ref[...].astype(f32)
    kinetic_ref[...] = kinetic_of(miller, lengths_ref[...])
    other = core_bands(fields_ref, place_ref[:, 1:2])
    other_ref[...] = other
    fields = [field_pair(own_ref[...]), field_pair(other)]
    both_ref[...] = both_weights(template_ref[...])
    double_ref[...] = double_weights(template_ref[...])
    weights = [own_both_ref, both_ref]

    def step(block, carry):
        base = pl.multiple_of(block * CHUNK, CHUNK)
        chunk = pl.ds(base, CHUNK)
        cosine, sine = phases_of(table_ref[chunk, :], miller)
        cos_ref[chunk, :] = cosine
        sin_ref[chunk, :] = sine
        phases = [(own_cos_ref[chunk, :], own_sin_ref[chunk, :]), (cosine, sine)]
        size = CHUNK // 2
        select = select_ref[pl.ds(pl.multiple_of(block * size, size), size), :]
        project_chunk(base, phases, fields, weights, select, out_ref, wave_ref)
        return carry

    lax.fori_loop(0, cos_ref.shape[0] // CHUNK, step, 0)


def next_kernel(
    own_kinetic_ref, kinetic_ref, own_ref, other_ref, mine_ref, low_ref, high_ref, both_ref,
    own_weights_ref, weights_ref, own_cos_ref, own_sin_ref, cos_ref, sin_ref, select_ref,
    fields_out_ref, out_ref, wave_ref,
):
    own = own_kinetic_ref[...] * own_ref[...]
    own = own + ((mine_ref[0] + high_ref[0]) + (low_ref[1] + both_ref[1]))
    fields_out_ref[...] = own
    other = kinetic_ref[...] * other_ref[...]
    other = other + ((mine_ref[1] + high_ref[1]) + (low_ref[0] + both_ref[0]))
    fields = [field_pair(own), field_pair(other)]
    weights = [own_weights_ref, weights_ref]

    def step(block, carry):
        base = pl.multiple_of(block * CHUNK, CHUNK)
        chunk = pl.ds(base, CHUNK)
        phases = [
            (own_cos_ref[chunk, :], own_sin_ref[chunk, :]),
            (cos_ref[chunk, :], sin_ref[chunk, :]),
        ]
        size = CHUNK // 2
        select = select_ref[pl.ds(pl.multiple_of(block * size, size), size), :]
        project_chunk(base, phases, fields, weights, select, out_ref, wave_ref)
        return carry

    lax.fori_loop(0, cos_ref.shape[0] // CHUNK, step, 0)


def last_kernel(kinetic_ref, own_ref, mine_ref, low_ref, high_ref, both_ref, out_ref):
    total = kinetic_ref[...] * own_ref[...]
    out_ref[...] = total + ((mine_ref[0] + high_ref[...]) + (low_ref[...] + both_ref[...]))


def join_kernel(
    place_ref, once_ref, other_once_ref, twice_ref, other_twice_ref, once_out_ref, twice_out_ref
):
    core = place_ref[:, 1:2]
    for mine_ref, other_ref, out_ref in (
        (once_ref, other_once_ref, once_out_ref), (twice_ref, other_twice_ref, twice_out_ref)
    ):
        mine, other = mine_ref[...], other_ref[...]
        half = mine.shape[0] // 2
        first = jnp.where(core == 0, mine, other)
        second = jnp.where(core == 0, other, mine)
        parts = [first[:half, :], second[:half, :], first[half:, :], second[half:, :]]
        out_ref[...] = jnp.concatenate(parts, axis=0)


def potential_kernel(parts_ref, own_potential_ref, potential_ref, out_ref):
    summed = jnp.sum(parts_ref[...].astype(f32), axis=0)
    count = potential_ref.shape[0]
    rows = summed.shape[0] // (2 * count)
    half = rows // 2
    low = lax.broadcasted_iota(jnp.int32, (64, 128), 1) < 64
    results = []
    for pair in range(2 * count):
        source = own_potential_ref if pair < count else potential_ref
        blocks = []
        for part in range(2):
            matrices = source[pair % count, part].astype(f32)
            blocks.append(jnp.where(low, matrices, 0.0))
            blocks.append(jnp.where(low, 0.0, matrices))
        weights = jnp.concatenate(blocks, axis=0).astype(bf16)
        high, middle, lowest = three_parts(summed[pair * rows : (pair + 1) * rows, :])
        pieces = jnp.concatenate(
            [high.astype(f32), middle.astype(f32), lowest.astype(f32)], axis=0
        ).astype(bf16)
        product = dot(pieces, weights, NT)
        product = product[2 * rows :, :] + product[rows : 2 * rows, :] + product[:rows, :]
        real, imag = product[:, :128], product[:, 128:]
        results.append(real[:half, :] - imag[half:, :])
        results.append(real[half:, :] + imag[:half, :])
    applied = jnp.concatenate(results, axis=0).astype(bf16)
    out_ref[...] = jnp.broadcast_to(applied[None], out_ref.shape)


def return_kernel(
    applied_ref, own_weights_ref, weights_ref, own_cos_ref, own_sin_ref, cos_ref, sin_ref,
    select_ref, out_ref, stack_ref,
):
    atoms = cos_ref.shape[0]
    _, rows, waves = out_ref.shape
    half = rows // 2
    weights = [own_weights_ref, weights_ref]
    low = lax.broadcasted_iota(jnp.int32, (1, 128), 1) < 64
    zero = jnp.zeros((rows, waves), f32)

    def step(block, carry):
        base = pl.multiple_of(block * CHUNK, CHUNK)
        chunk = pl.ds(base, CHUNK)
        size = CHUNK // 2
        select = select_ref[pl.ds(pl.multiple_of(block * size, size), size), :]
        height = size * rows
        whole = applied_ref[pl.ds(pl.multiple_of(base // 2 * rows, height), height), :]
        whole = whole.astype(f32)
        for pair in range(size):
            applied = whole[pair * rows : (pair + 1) * rows, :]
            chosen = select[pair : pair + 1, :] > 0.5
            two = slice(2 * pair * rows, 2 * (pair + 1) * rows)
            for kind in range(2):
                take_even = low & chosen if kind == 0 else low & ~chosen
                take_odd = ~low & ~chosen if kind == 0 else ~low & chosen
                split = jnp.concatenate(
                    [jnp.where(take_even, applied, 0.0), jnp.where(take_odd, applied, 0.0)], axis=0
                )
                stack_ref[two, kind * 128 : (kind + 1) * 128] = split.astype(bf16)
        sums = []
        for side, (cosines, sines) in enumerate(((own_cos_ref, own_sin_ref), (cos_ref, sin_ref))):
            straight, turned = carry[side]
            cosine, sine = cosines[chunk, :], sines[chunk, :]
            images = dot(stack_ref[...], weights[side][...], NN)
            for atom in range(CHUNK):
                image = images[atom * rows : (atom + 1) * rows, :]
                straight = straight + cosine[atom : atom + 1, :] * image
                turned = turned + sine[atom : atom + 1, :] * image
            sums.append((straight, turned))
        return tuple(sums)

    sums = lax.fori_loop(0, atoms // CHUNK, step, ((zero, zero), (zero, zero)))
    for side, (straight, turned) in enumerate(sums):
        real = straight[:half, :] + turned[half:, :]
        imag = straight[half:, :] - turned[:half, :]
        out_ref[side] = jnp.concatenate([real, imag], axis=0)


def vmem(count):
    return [pl.BlockSpec(memory_space=pltpu.VMEM)] * count


def shape(dims, dtype):
    return jax.ShapeDtypeStruct(dims, dtype)


def call(kernel, args, out_shape, name, scratch_shapes=()):
    return pl.pallas_call(
        kernel,
        in_specs=vmem(len(args)),
        out_specs=tuple(vmem(len(out_shape))),
        out_shape=tuple(out_shape),
        scratch_shapes=scratch_shapes,
        compiler_params=LIMIT,
        name=name,
    )(*args)


def flip(array, *axes):
    pairs = [(place, 2 ** len(axes) - 1 - place) for place in range(2 ** len(axes))]
    return lax.ppermute(array, axes, pairs)


def per_device(bands_in, template, potential, miller, positions, species, atom_order, reciprocal):
    plane = lax.axis_size("zx")
    groups = lax.axis_size("yh") * lax.axis_size("core")
    slot_dev = potential.shape[0]
    atoms = 2 * slot_dev * plane
    species_count, harmonics, waves = template.shape
    bands = bands_in.shape[1]
    rows = bands
    pairs = slot_dev // 2
    message = 2 * pairs * rows
    width = 2 * harmonics
    template = template.reshape(species_count * harmonics, waves)
    fields = bands_in.reshape(2 * bands, waves)
    matrices = potential.reshape(pairs, 2, 2, harmonics, harmonics)
    matrices = matrices.transpose(0, 2, 3, 1, 4).reshape(pairs, 2, harmonics, width)
    core = lax.axis_index("core")
    stride = groups * slot_dev
    first_slot = lax.axis_index("yl") * plane * stride + lax.axis_index("yh") * 2 * slot_dev
    place = jnp.stack([first_slot, core]).astype(jnp.int32).reshape(1, 2)
    lengths = reciprocal.reshape(1, 3)
    coefs_shape = shape((atoms // 2 * rows, width), bf16)
    fields_shape = shape((rows, waves), f32)
    whole_shape = shape((2 * bands, waves), f32)
    phase_shape = shape((atoms, waves), f32)
    kinetic_shape = shape((1, waves), f32)
    weights_shape = shape((2 * width, waves), bf16)
    wave_scratch = pltpu.VMEM((2, CHUNK * rows, waves), bf16)

    other_miller = flip(miller, "yl")
    other_fields = flip(fields, "yl")
    other_template = flip(template, "yl")
    own_cos, own_sin, select, table, own, own_kinetic, own_both, own_double = call(
        functools.partial(prepare_kernel, stride, slot_dev),
        (
            place, lengths, miller, positions, species.reshape(1, -1), atom_order.reshape(1, -1),
            fields, template,
        ),
        (
            phase_shape, phase_shape, shape((atoms // 2, 128), f32), shape((atoms, 16), f32),
            fields_shape, kinetic_shape, weights_shape, weights_shape,
        ),
        "prepare",
    )
    coefs, other_cos, other_sin, other, other_kinetic, other_both, other_double = call(
        first_kernel,
        (
            place, lengths, table, other_miller, own, other_fields, own_both, other_template,
            own_cos, own_sin, select,
        ),
        (
            coefs_shape, phase_shape, phase_shape, fields_shape, kinetic_shape, weights_shape,
            weights_shape,
        ),
        "first",
        [wave_scratch],
    )
    other_matrices = flip(matrices, "core")
    phases = (own_cos, own_sin, other_cos, other_sin, select)

    def return_fields(coefs):
        parts = lax.all_to_all(coefs.reshape(plane, message, width), "zx", 0, 0, tiled=True)
        (applied,) = call(
            potential_kernel,
            (parts, matrices, other_matrices),
            (shape((plane, message, width), bf16),),
            "potential",
        )
        applied = lax.all_to_all(applied, "zx", 0, 0, tiled=True)
        (mine,) = call(
            return_kernel,
            (applied.reshape(atoms // 2 * rows, width), own_double, other_double) + phases,
            (shape((2, rows, waves), f32),),
            "back",
            [pltpu.VMEM((CHUNK * rows, 2 * width), bf16)],
        )
        return mine

    mine = return_fields(coefs)
    once, coefs = call(
        next_kernel,
        (
            own_kinetic, other_kinetic, own, other, mine, flip(mine, "yl"), flip(mine, "yh"),
            flip(mine, "yl", "yh"), own_both, other_both,
        )
        + phases,
        (fields_shape, coefs_shape),
        "next",
        [wave_scratch],
    )
    other_once = flip(once, "core")
    mine = return_fields(coefs)
    (twice,) = call(
        last_kernel,
        (
            own_kinetic, once, mine, flip(mine[1], "yl"), flip(mine[0], "yh"),
            flip(mine[1], "yl", "yh"),
        ),
        (fields_shape,),
        "last",
    )
    once, twice = call(
        join_kernel,
        (place, once, other_once, twice, flip(twice, "core")),
        (whole_shape, whole_shape),
        "join",
    )
    return once.reshape(bands_in.shape), twice.reshape(bands_in.shape)


def solution(mesh):
    pw, groups = mesh.devices.shape
    fine = Mesh(mesh.devices.reshape(2, pw // 2, 2, groups // 2), ("yl", "zx", "yh", "core"))
    waves, slots = ("yl", "zx"), ("yl", "zx", "yh", "core")
    in_specs = (
        P(None, None, waves),
        P(None, None, waves),
        P(slots, None),
        P(None, waves),
        P(),
        P(),
        P(),
        P(),
    )
    out_specs = (P(None, None, waves), P(None, None, waves))
    return jax.shard_map(
        per_device, mesh=fine, in_specs=in_specs, out_specs=out_specs, check_vma=False
    )
```

```python
import functools

import jax
import jax.numpy as jnp
from jax import lax
from jax.experimental import pallas as pl
from jax.experimental.pallas import tpu as pltpu
from jax.sharding import Mesh
from jax.sharding import PartitionSpec as P

f32 = jnp.float32
bf16 = jnp.bfloat16

COS_TURN = (
    0.9999999890590225,
    -19.739204499453912,
    64.93911745989556,
    -85.45013953088248,
    60.167630950949295,
    -25.96759924849463,
    6.528658161366808,
)
SIN_TURN = (
    6.283185302511503,
    -41.34170040531749,
    81.60513138579344,
    -76.70301535379849,
    42.02592698556796,
    -14.899846667364866,
    3.238137509743233,
)
NT = (((1,), (1,)), ((), ()))
NN = (((1,), (0,)), ((), ()))
CHUNK = 128
STEP = 128
LIMIT = pltpu.CompilerParams(vmem_limit_bytes=12 * 2**20)


def dot(left, right, dims):
    return lax.dot_general(left, right, dims, preferred_element_type=f32)


def horner(coefs, arg):
    total = jnp.full_like(arg, coefs[-1])
    for coef in coefs[-2::-1]:
        total = total * arg + coef
    return total


def three_parts(values):
    high = values.astype(bf16)
    rest = values - high.astype(f32)
    middle = rest.astype(bf16)
    low = (rest - middle.astype(f32)).astype(bf16)
    return high, middle, low


def atom_table(positions, species, order, first_slot, core, rows, stride, slot_dev):
    atoms = order.shape[1]
    row = lax.broadcasted_iota(jnp.int32, (rows, 1), 0)
    pair = 2 * slot_dev
    side = (row % pair // slot_dev) ^ core
    slot = first_slot + row // pair * stride + side * slot_dev + row % slot_dev
    lane = lax.broadcasted_iota(jnp.int32, (rows, atoms), 1)
    pick_slot = jnp.where(lane == slot, 1.0, 0.0).astype(bf16)
    coarse, fine = order // 128, order % 128
    pad = jnp.zeros((14, atoms), f32)
    digits = jnp.concatenate([coarse.astype(f32), fine.astype(f32), pad], axis=0).astype(bf16)
    found = dot(pick_slot, digits, NT)
    atom = (found[:, 0:1] * 128.0 + found[:, 1:2]).astype(jnp.int32)
    pick_atom = jnp.where(lane == atom, 1.0, 0.0).astype(bf16)
    high, middle, low = three_parts(positions)
    pad = jnp.zeros((6, atoms), bf16)
    facts = jnp.concatenate([high, middle, low, species.astype(f32).astype(bf16), pad], axis=0)
    return dot(pick_atom, facts, NT)


def field_pair(fields):
    half = fields.shape[0] // 2
    return fields, jnp.concatenate([-fields[half:, :], fields[:half, :]], axis=0)


def core_bands(fields_ref, core):
    quarter = fields_ref.shape[0] // 4
    parts = [fields_ref[part * quarter : (part + 1) * quarter, :] for part in range(4)]
    first = jnp.concatenate([parts[0], parts[2]], axis=0)
    second = jnp.concatenate([parts[1], parts[3]], axis=0)
    return jnp.where(core == 0, first, second)


def phases_of(table, miller):
    turns = jnp.zeros((table.shape[0], miller.shape[1]), f32)
    for axis in range(3):
        centre = table[:, axis : axis + 1] + table[:, 3 + axis : 4 + axis]
        centre = centre + table[:, 6 + axis : 7 + axis]
        turns = turns + centre * miller[axis : axis + 1, :]
    turns = turns - jnp.round(turns)
    square = turns * turns
    return horner(COS_TURN, square), turns * horner(SIN_TURN, square)


def kinetic_of(miller, lengths):
    total = jnp.zeros((1, miller.shape[1]), f32)
    for axis in range(3):
        wave_number = lengths[:, axis : axis + 1] * miller[axis : axis + 1, :]
        total = total + wave_number * wave_number
    return 0.5 * total


def both_weights(template):
    low, high = template[:64, :], template[64:, :]
    return jnp.concatenate([low, high, high, low], axis=0)


def double_weights(template):
    low, high = template[:64, :], template[64:, :]
    return jnp.concatenate([low, low, high, high], axis=0)


def prepare_kernel(
    stride, slot_dev, place_ref, *refs,
):
    sources, refs = refs[:7], refs[7:]
    cos_ref, sin_ref, select_ref, table_ref, own_ref, kinetic_ref, both_ref, kept_ref = refs[:8]
    targets, semaphores = refs[8:15], refs[15]
    copies = [
        pltpu.make_async_copy(source, target, semaphores.at[number])
        for number, (source, target) in enumerate(zip(sources, targets))
    ]
    for copy in copies:
        copy.start()
    for copy in copies:
        copy.wait()
    order_ref, positions_ref, species_ref, miller_ref = targets[:4]
    lengths_ref, fields_ref, template_ref = targets[4:]
    kept_ref[...] = lengths_ref[...]
    atoms = cos_ref.shape[0]
    core = place_ref[:, 1:2]
    table_ref[...] = atom_table(
        positions_ref[...], species_ref[...], order_ref[...], place_ref[:, 0:1], core, atoms,
        stride, slot_dev,
    )
    miller = miller_ref[...].astype(f32)
    kinetic_ref[...] = kinetic_of(miller, lengths_ref[...])
    own_ref[...] = core_bands(fields_ref, core)
    both_ref[...] = both_weights(template_ref[...])
    low = lax.broadcasted_iota(jnp.int32, (1, 128), 1) < 64

    def step(block, carry):
        base = pl.multiple_of(block * STEP, STEP)
        table = table_ref[pl.ds(base, STEP), :]
        cosine, sine = phases_of(table, miller)
        cos_ref[pl.ds(base, STEP), :] = cosine
        sin_ref[pl.ds(base, STEP), :] = sine
        kinds = table[:, 9:10]
        picked = []
        for pair in range(STEP // 2):
            even = 1.0 - kinds[2 * pair : 2 * pair + 1, :]
            odd = kinds[2 * pair + 1 : 2 * pair + 2, :]
            picked.append(jnp.where(low, even, odd))
        half = pl.ds(pl.multiple_of(block * (STEP // 2), STEP // 2), STEP // 2)
        select_ref[half, :] = jnp.concatenate(picked, axis=0)
        return carry

    lax.fori_loop(0, atoms // STEP, step, 0)


def project_chunk(base, phases, fields, weights, select, out_ref, wave_ref):
    rows = fields[0][0].shape[0]
    products = []
    for side in range(2):
        cosine, sine = phases[side]
        straight, turned = fields[side]
        for pair in range(CHUNK // 2):
            waves = [
                cosine[atom : atom + 1, :] * straight + sine[atom : atom + 1, :] * turned
                for atom in (2 * pair, 2 * pair + 1)
            ]
            two = slice(2 * pair * rows, 2 * (pair + 1) * rows)
            wave_ref[side, two, :] = jnp.concatenate(waves, axis=0).astype(bf16)
        products.append(dot(wave_ref[side], weights[side][...], NT))
    both = products[0] + products[1]
    low = lax.broadcasted_iota(jnp.int32, (rows, 128), 1) < 64
    results = []
    for pair in range(CHUNK // 2):
        even = both[2 * pair * rows : (2 * pair + 1) * rows, :]
        odd = both[(2 * pair + 1) * rows : (2 * pair + 2) * rows, :]
        first = jnp.where(low, even[:, :128], odd[:, :128])
        second = jnp.where(low, even[:, 128:], odd[:, 128:])
        results.append(jnp.where(select[pair : pair + 1, :] > 0.5, first, second))
    size = CHUNK // 2 * rows
    start = pl.multiple_of(base // 2 * rows, size)
    out_ref[pl.ds(start, size), :] = jnp.concatenate(results, axis=0).astype(bf16)


def first_kernel(
    place_ref, lengths_ref, table_ref, miller_ref, own_ref, fields_ref, own_both_ref,
    template_ref, own_cos_ref, own_sin_ref, select_ref, out_ref, cos_ref, sin_ref, other_ref,
    kinetic_ref, both_ref, wave_ref,
):
    miller = miller_ref[...].astype(f32)
    kinetic_ref[...] = kinetic_of(miller, lengths_ref[...])
    other = core_bands(fields_ref, place_ref[:, 1:2])
    other_ref[...] = other
    fields = [field_pair(own_ref[...]), field_pair(other)]
    both_ref[...] = both_weights(template_ref[...])
    weights = [own_both_ref, both_ref]

    def step(block, carry):
        base = pl.multiple_of(block * CHUNK, CHUNK)
        chunk = pl.ds(base, CHUNK)
        cosine, sine = phases_of(table_ref[chunk, :], miller)
        cos_ref[chunk, :] = cosine
        sin_ref[chunk, :] = sine
        phases = [(own_cos_ref[chunk, :], own_sin_ref[chunk, :]), (cosine, sine)]
        size = CHUNK // 2
        select = select_ref[pl.ds(pl.multiple_of(block * size, size), size), :]
        project_chunk(base, phases, fields, weights, select, out_ref, wave_ref)
        return carry

    lax.fori_loop(0, cos_ref.shape[0] // CHUNK, step, 0)


def next_kernel(
    own_kinetic_ref, kinetic_ref, own_ref, other_ref, near_ref, far_ref,
    own_weights_ref, weights_ref, own_cos_ref, own_sin_ref, cos_ref, sin_ref, select_ref,
    fields_out_ref, out_ref, wave_ref,
):
    own = own_kinetic_ref[...] * own_ref[...]
    own = own + (near_ref[0] + far_ref[1])
    fields_out_ref[...] = own
    other = kinetic_ref[...] * other_ref[...]
    other = other + (near_ref[1] + far_ref[0])
    fields = [field_pair(own), field_pair(other)]
    weights = [own_weights_ref, weights_ref]

    def step(block, carry):
        base = pl.multiple_of(block * CHUNK, CHUNK)
        chunk = pl.ds(base, CHUNK)
        phases = [
            (own_cos_ref[chunk, :], own_sin_ref[chunk, :]),
            (cos_ref[chunk, :], sin_ref[chunk, :]),
        ]
        size = CHUNK // 2
        select = select_ref[pl.ds(pl.multiple_of(block * size, size), size), :]
        project_chunk(base, phases, fields, weights, select, out_ref, wave_ref)
        return carry

    lax.fori_loop(0, cos_ref.shape[0] // CHUNK, step, 0)


def near_kernel(mine_ref, low_ref, out_ref):
    out_ref[0] = mine_ref[0] + low_ref[1]
    out_ref[1] = mine_ref[1] + low_ref[0]


def last_kernel(kinetic_ref, own_ref, near_ref, far_ref, out_ref):
    out_ref[0] = own_ref[...]
    out_ref[1] = kinetic_ref[...] * own_ref[...] + (near_ref[0] + far_ref[...])


def join_kernel(place_ref, mine_ref, other_ref, once_ref, twice_ref):
    core = place_ref[:, 1:2]
    for number, out_ref in enumerate((once_ref, twice_ref)):
        mine, other = mine_ref[number], other_ref[number]
        half = mine.shape[0] // 2
        first = jnp.where(core == 0, mine, other)
        second = jnp.where(core == 0, other, mine)
        parts = [first[:half, :], second[:half, :], first[half:, :], second[half:, :]]
        out_ref[...] = jnp.concatenate(parts, axis=0)


def potential_kernel(parts_ref, own_potential_ref, potential_ref, out_ref):
    summed = jnp.sum(parts_ref[...].astype(f32), axis=0)
    count = potential_ref.shape[0]
    rows = summed.shape[0] // (2 * count)
    half = rows // 2
    low = lax.broadcasted_iota(jnp.int32, (64, 128), 1) < 64
    results = []
    for pair in range(2 * count):
        source = own_potential_ref if pair < count else potential_ref
        blocks = []
        for part in range(2):
            matrices = source[pair % count, part].astype(f32)
            blocks.append(jnp.where(low, matrices, 0.0))
            blocks.append(jnp.where(low, 0.0, matrices))
        weights = jnp.concatenate(blocks, axis=0).astype(bf16)
        high, middle, lowest = three_parts(summed[pair * rows : (pair + 1) * rows, :])
        pieces = jnp.concatenate(
            [high.astype(f32), middle.astype(f32), lowest.astype(f32)], axis=0
        ).astype(bf16)
        product = dot(pieces, weights, NT)
        product = product[2 * rows :, :] + product[rows : 2 * rows, :] + product[:rows, :]
        real, imag = product[:, :128], product[:, 128:]
        results.append(real[:half, :] - imag[half:, :])
        results.append(real[half:, :] + imag[:half, :])
    applied = jnp.concatenate(results, axis=0).astype(bf16)
    out_ref[...] = jnp.broadcast_to(applied[None], out_ref.shape)


def return_kernel(
    applied_ref, own_template_ref, template_ref, own_cos_ref, own_sin_ref, cos_ref, sin_ref,
    select_ref, out_ref, stack_ref,
):
    atoms = cos_ref.shape[0]
    _, rows, waves = out_ref.shape
    half = rows // 2
    weights = [double_weights(own_template_ref[...]), double_weights(template_ref[...])]
    low = lax.broadcasted_iota(jnp.int32, (1, 128), 1) < 64
    zero = jnp.zeros((rows, waves), f32)

    def step(block, carry):
        base = pl.multiple_of(block * CHUNK, CHUNK)
        chunk = pl.ds(base, CHUNK)
        size = CHUNK // 2
        select = select_ref[pl.ds(pl.multiple_of(block * size, size), size), :]
        height = size * rows
        whole = applied_ref[pl.ds(pl.multiple_of(base // 2 * rows, height), height), :]
        whole = whole.astype(f32)
        for pair in range(size):
            applied = whole[pair * rows : (pair + 1) * rows, :]
            chosen = select[pair : pair + 1, :] > 0.5
            two = slice(2 * pair * rows, 2 * (pair + 1) * rows)
            for kind in range(2):
                take_even = low & chosen if kind == 0 else low & ~chosen
                take_odd = ~low & ~chosen if kind == 0 else ~low & chosen
                split = jnp.concatenate(
                    [jnp.where(take_even, applied, 0.0), jnp.where(take_odd, applied, 0.0)], axis=0
                )
                stack_ref[two, kind * 128 : (kind + 1) * 128] = split.astype(bf16)
        sums = []
        for side, (cosines, sines) in enumerate(((own_cos_ref, own_sin_ref), (cos_ref, sin_ref))):
            straight, turned = carry[side]
            cosine, sine = cosines[chunk, :], sines[chunk, :]
            images = dot(stack_ref[...], weights[side], NN)
            for atom in range(CHUNK):
                image = images[atom * rows : (atom + 1) * rows, :]
                straight = straight + cosine[atom : atom + 1, :] * image
                turned = turned + sine[atom : atom + 1, :] * image
            sums.append((straight, turned))
        return tuple(sums)

    sums = lax.fori_loop(0, atoms // CHUNK, step, ((zero, zero), (zero, zero)))
    for side, (straight, turned) in enumerate(sums):
        real = straight[:half, :] + turned[half:, :]
        imag = straight[half:, :] - turned[:half, :]
        out_ref[side] = jnp.concatenate([real, imag], axis=0)


def vmem(count):
    return [pl.BlockSpec(memory_space=pltpu.VMEM)] * count


def shape(dims, dtype):
    return jax.ShapeDtypeStruct(dims, dtype)


def call(kernel, args, out_shape, name, scratch_shapes=(), unread=0):
    return pl.pallas_call(
        kernel,
        in_specs=vmem(len(args) - unread) + [pl.BlockSpec(memory_space=pltpu.HBM)] * unread,
        out_specs=tuple(vmem(len(out_shape))),
        out_shape=tuple(out_shape),
        scratch_shapes=scratch_shapes,
        compiler_params=LIMIT,
        name=name,
    )(*args)


def flip(array, *axes):
    pairs = [(place, 2 ** len(axes) - 1 - place) for place in range(2 ** len(axes))]
    return lax.ppermute(array, axes, pairs)


def per_device(bands_in, template, potential, miller, positions, species, atom_order, reciprocal):
    plane = lax.axis_size("zx")
    groups = lax.axis_size("yh") * lax.axis_size("core")
    slot_dev = potential.shape[0]
    atoms = 2 * slot_dev * plane
    species_count, harmonics, waves = template.shape
    bands = bands_in.shape[1]
    rows = bands
    pairs = slot_dev // 2
    message = 2 * pairs * rows
    width = 2 * harmonics
    template = template.reshape(species_count * harmonics, waves)
    fields = bands_in.reshape(2 * bands, waves)
    matrices = potential.reshape(pairs, 2, 2, harmonics, harmonics)
    matrices = matrices.transpose(0, 2, 3, 1, 4).reshape(pairs, 2, harmonics, width)
    core = lax.axis_index("core")
    stride = groups * slot_dev
    first_slot = lax.axis_index("yl") * plane * stride + lax.axis_index("yh") * 2 * slot_dev
    place = jnp.stack([first_slot, core]).astype(jnp.int32).reshape(1, 2)
    lengths = reciprocal.reshape(1, 3)
    coefs_shape = shape((atoms // 2 * rows, width), bf16)
    fields_shape = shape((rows, waves), f32)
    whole_shape = shape((2 * bands, waves), f32)
    phase_shape = shape((atoms, waves), f32)
    kinetic_shape = shape((1, waves), f32)
    weights_shape = shape((2 * width, waves), bf16)
    wave_scratch = pltpu.VMEM((2, CHUNK * rows, waves), bf16)

    other_miller = flip(miller, "yl")
    other_fields = flip(fields, "yl")
    other_template = flip(template, "yl")
    inputs = (
        atom_order.reshape(1, -1), positions, species.reshape(1, -1), miller, lengths, fields,
        template,
    )
    inputs = tuple(pltpu.with_memory_space_constraint(value, pltpu.HBM) for value in inputs)
    own_cos, own_sin, select, table, own, own_kinetic, own_both, lengths = call(
        functools.partial(prepare_kernel, stride, slot_dev),
        (place,) + inputs,
        (
            phase_shape, phase_shape, shape((atoms // 2, 128), f32), shape((atoms, 16), f32),
            fields_shape, kinetic_shape, weights_shape, shape(lengths.shape, f32),
        ),
        "prepare",
        [pltpu.VMEM(value.shape, value.dtype) for value in inputs]
        + [pltpu.SemaphoreType.DMA((len(inputs),))],
        unread=len(inputs),
    )
    coefs, other_cos, other_sin, other, other_kinetic, other_both = call(
        first_kernel,
        (
            place, lengths, table, other_miller, own, other_fields, own_both, other_template,
            own_cos, own_sin, select,
        ),
        (
            coefs_shape, phase_shape, phase_shape, fields_shape, kinetic_shape, weights_shape,
        ),
        "first",
        [wave_scratch],
    )
    other_matrices = flip(matrices, "core")
    phases = (own_cos, own_sin, other_cos, other_sin, select)

    def return_fields(coefs):
        parts = lax.all_to_all(coefs.reshape(plane, message, width), "zx", 0, 0, tiled=True)
        (applied,) = call(
            potential_kernel,
            (parts, matrices, other_matrices),
            (shape((plane, message, width), bf16),),
            "potential",
        )
        applied = lax.all_to_all(applied, "zx", 0, 0, tiled=True)
        (mine,) = call(
            return_kernel,
            (applied.reshape(atoms // 2 * rows, width), template, other_template) + phases,
            (shape((2, rows, waves), f32),),
            "back",
            [pltpu.VMEM((CHUNK * rows, 2 * width), bf16)],
        )
        (near,) = call(
            near_kernel, (mine, flip(mine, "yl")), (shape((2, rows, waves), f32),), "near"
        )
        return near

    near = return_fields(coefs)
    once, coefs = call(
        next_kernel,
        (
            own_kinetic, other_kinetic, own, other, near, flip(near, "yl", "yh"), own_both,
            other_both,
        )
        + phases,
        (fields_shape, coefs_shape),
        "next",
        [wave_scratch],
    )
    near = return_fields(coefs)
    (mine,) = call(
        last_kernel,
        (own_kinetic, once, near, flip(near[1], "yl", "yh")),
        (shape((2, rows, waves), f32),),
        "last",
    )
    once, twice = call(
        join_kernel, (place, mine, flip(mine, "core")), (whole_shape, whole_shape), "join"
    )
    return once.reshape(bands_in.shape), twice.reshape(bands_in.shape)


def solution(mesh):
    pw, groups = mesh.devices.shape
    fine = Mesh(mesh.devices.reshape(2, pw // 2, 2, groups // 2), ("yl", "zx", "yh", "core"))
    waves, slots = ("yl", "zx"), ("yl", "zx", "yh", "core")
    in_specs = (
        P(None, None, waves),
        P(None, None, waves),
        P(slots, None),
        P(None, waves),
        P(),
        P(),
        P(),
        P(),
    )
    out_specs = (P(None, None, waves), P(None, None, waves))
    return jax.shard_map(
        per_device, mesh=fine, in_specs=in_specs, out_specs=out_specs, check_vma=False
    )
```

```python
import functools

import jax
import jax.numpy as jnp
from jax import lax
from jax.experimental import pallas as pl
from jax.experimental.pallas import tpu as pltpu
from jax.sharding import Mesh
from jax.sharding import PartitionSpec as P

f32 = jnp.float32
bf16 = jnp.bfloat16

COS_TURN = (
    0.9999992107823212,
    -19.738980355764024,
    64.92865742103461,
    -85.27162153431523,
    58.790492120199225,
    -21.07110562773966,
)
SIN_TURN = (
    6.283184916495427,
    -41.34158923268859,
    81.59994332978516,
    -76.61447253128296,
    41.342882354732154,
    -12.471243535293539,
)
NT = (((1,), (1,)), ((), ()))
NN = (((1,), (0,)), ((), ()))
CHUNK = 128
STEP = 256
LIMIT = pltpu.CompilerParams(vmem_limit_bytes=12 * 2**20)


def dot(left, right, dims):
    return lax.dot_general(left, right, dims, preferred_element_type=f32)


def horner(coefs, arg):
    total = jnp.full_like(arg, coefs[-1])
    for coef in coefs[-2::-1]:
        total = total * arg + coef
    return total


def three_parts(values):
    high = values.astype(bf16)
    rest = values - high.astype(f32)
    middle = rest.astype(bf16)
    low = (rest - middle.astype(f32)).astype(bf16)
    return high, middle, low


def atom_table(positions, species, order, first_slot, core, rows, stride, slot_dev):
    atoms = order.shape[1]
    row = lax.broadcasted_iota(jnp.int32, (rows, 1), 0)
    pair = 2 * slot_dev
    side = (row % pair // slot_dev) ^ core
    slot = first_slot + row // pair * stride + side * slot_dev + row % slot_dev
    lane = lax.broadcasted_iota(jnp.int32, (rows, atoms), 1)
    pick_slot = jnp.where(lane == slot, 1.0, 0.0).astype(bf16)
    coarse, fine = order // 128, order % 128
    pad = jnp.zeros((14, atoms), f32)
    digits = jnp.concatenate([coarse.astype(f32), fine.astype(f32), pad], axis=0).astype(bf16)
    found = dot(pick_slot, digits, NT)
    atom = (found[:, 0:1] * 128.0 + found[:, 1:2]).astype(jnp.int32)
    pick_atom = jnp.where(lane == atom, 1.0, 0.0).astype(bf16)
    high, middle, low = three_parts(positions)
    pad = jnp.zeros((6, atoms), bf16)
    facts = jnp.concatenate([high, middle, low, species.astype(f32).astype(bf16), pad], axis=0)
    return dot(pick_atom, facts, NT)


def field_pair(fields):
    half = fields.shape[0] // 2
    return fields, jnp.concatenate([-fields[half:, :], fields[:half, :]], axis=0)


def core_bands(fields_ref, core):
    quarter = fields_ref.shape[0] // 4
    parts = [fields_ref[part * quarter : (part + 1) * quarter, :] for part in range(4)]
    first = jnp.concatenate([parts[0], parts[2]], axis=0)
    second = jnp.concatenate([parts[1], parts[3]], axis=0)
    return jnp.where(core == 0, first, second)


def phases_of(table, miller):
    turns = jnp.zeros((table.shape[0], miller.shape[1]), f32)
    for axis in range(3):
        centre = table[:, axis : axis + 1] + table[:, 3 + axis : 4 + axis]
        centre = centre + table[:, 6 + axis : 7 + axis]
        turns = turns + centre * miller[axis : axis + 1, :]
    turns = turns - jnp.round(turns)
    square = turns * turns
    return horner(COS_TURN, square), turns * horner(SIN_TURN, square)


def kinetic_of(miller, lengths):
    total = jnp.zeros((1, miller.shape[1]), f32)
    for axis in range(3):
        wave_number = lengths[:, axis : axis + 1] * miller[axis : axis + 1, :]
        total = total + wave_number * wave_number
    return 0.5 * total


def both_weights(template):
    low, high = template[:64, :], template[64:, :]
    return jnp.concatenate([low, high, high, low], axis=0)


def double_weights(template):
    low, high = template[:64, :], template[64:, :]
    return jnp.concatenate([low, low, high, high], axis=0)


def prepare_kernel(
    stride, slot_dev, place_ref, *refs,
):
    sources, refs = refs[:7], refs[7:]
    cos_ref, sin_ref, select_ref, table_ref, own_ref, kinetic_ref, both_ref, kept_ref = refs[:8]
    targets, semaphores = refs[8:15], refs[15]
    copies = [
        pltpu.make_async_copy(source, target, semaphores.at[number])
        for number, (source, target) in enumerate(zip(sources, targets))
    ]
    for copy in copies:
        copy.start()
    for copy in copies[:5]:
        copy.wait()
    order_ref, positions_ref, species_ref, miller_ref = targets[:4]
    lengths_ref, fields_ref, template_ref = targets[4:]
    kept_ref[...] = lengths_ref[...]
    atoms = cos_ref.shape[0]
    core = place_ref[:, 1:2]
    table_ref[...] = atom_table(
        positions_ref[...], species_ref[...], order_ref[...], place_ref[:, 0:1], core, atoms,
        stride, slot_dev,
    )
    miller = miller_ref[...].astype(f32)
    kinetic_ref[...] = kinetic_of(miller, lengths_ref[...])
    low = lax.broadcasted_iota(jnp.int32, (1, 128), 1) < 64

    def step(block, carry):
        base = pl.multiple_of(block * STEP, STEP)
        table = table_ref[pl.ds(base, STEP), :]
        cosine, sine = phases_of(table, miller)
        cos_ref[pl.ds(base, STEP), :] = cosine
        sin_ref[pl.ds(base, STEP), :] = sine
        kinds = table[:, 9:10]
        picked = []
        for pair in range(STEP // 2):
            even = 1.0 - kinds[2 * pair : 2 * pair + 1, :]
            odd = kinds[2 * pair + 1 : 2 * pair + 2, :]
            picked.append(jnp.where(low, even, odd))
        half = pl.ds(pl.multiple_of(block * (STEP // 2), STEP // 2), STEP // 2)
        select_ref[half, :] = jnp.concatenate(picked, axis=0)
        return carry

    lax.fori_loop(0, atoms // STEP, step, 0)
    for copy in copies[5:]:
        copy.wait()
    own_ref[...] = core_bands(fields_ref, core)
    both_ref[...] = both_weights(template_ref[...])


def project_chunk(base, phases, fields, weights, select, out_ref, wave_ref):
    rows = fields[0][0].shape[0]
    products = []
    for side in range(2):
        cosine, sine = phases[side]
        straight, turned = fields[side]
        for pair in range(CHUNK // 2):
            waves = [
                cosine[atom : atom + 1, :] * straight + sine[atom : atom + 1, :] * turned
                for atom in (2 * pair, 2 * pair + 1)
            ]
            two = slice(2 * pair * rows, 2 * (pair + 1) * rows)
            wave_ref[side, two, :] = jnp.concatenate(waves, axis=0).astype(bf16)
        products.append(dot(wave_ref[side], weights[side][...], NT))
    both = products[0] + products[1]
    low = lax.broadcasted_iota(jnp.int32, (rows, 128), 1) < 64
    results = []
    for pair in range(CHUNK // 2):
        even = both[2 * pair * rows : (2 * pair + 1) * rows, :]
        odd = both[(2 * pair + 1) * rows : (2 * pair + 2) * rows, :]
        first = jnp.where(low, even[:, :128], odd[:, :128])
        second = jnp.where(low, even[:, 128:], odd[:, 128:])
        results.append(jnp.where(select[pair : pair + 1, :] > 0.5, first, second))
    size = CHUNK // 2 * rows
    start = pl.multiple_of(base // 2 * rows, size)
    out_ref[pl.ds(start, size), :] = jnp.concatenate(results, axis=0).astype(bf16)


def first_kernel(
    place_ref, lengths_ref, table_ref, miller_ref, own_ref, fields_ref, own_both_ref,
    template_ref, own_cos_ref, own_sin_ref, select_ref, _matrices_ref, _other_matrices_ref,
    out_ref, cos_ref, sin_ref, other_ref,
    kinetic_ref, both_ref, wave_ref,
):
    miller = miller_ref[...].astype(f32)
    kinetic_ref[...] = kinetic_of(miller, lengths_ref[...])
    other = core_bands(fields_ref, place_ref[:, 1:2])
    other_ref[...] = other
    fields = [field_pair(own_ref[...]), field_pair(other)]
    both_ref[...] = both_weights(template_ref[...])
    weights = [own_both_ref, both_ref]

    def step(block, carry):
        base = pl.multiple_of(block * CHUNK, CHUNK)
        chunk = pl.ds(base, CHUNK)
        cosine, sine = phases_of(table_ref[chunk, :], miller)
        cos_ref[chunk, :] = cosine
        sin_ref[chunk, :] = sine
        phases = [(own_cos_ref[chunk, :], own_sin_ref[chunk, :]), (cosine, sine)]
        size = CHUNK // 2
        select = select_ref[pl.ds(pl.multiple_of(block * size, size), size), :]
        project_chunk(base, phases, fields, weights, select, out_ref, wave_ref)
        return carry

    lax.fori_loop(0, cos_ref.shape[0] // CHUNK, step, 0)


def next_kernel(
    own_kinetic_ref, kinetic_ref, own_ref, other_ref, near_ref, far_ref,
    own_weights_ref, weights_ref, own_cos_ref, own_sin_ref, cos_ref, sin_ref, select_ref,
    fields_out_ref, out_ref, wave_ref,
):
    own = own_kinetic_ref[...] * own_ref[...]
    own = own + (near_ref[0] + far_ref[1])
    fields_out_ref[...] = own
    other = kinetic_ref[...] * other_ref[...]
    other = other + (near_ref[1] + far_ref[0])
    fields = [field_pair(own), field_pair(other)]
    weights = [own_weights_ref, weights_ref]

    def step(block, carry):
        base = pl.multiple_of(block * CHUNK, CHUNK)
        chunk = pl.ds(base, CHUNK)
        phases = [
            (own_cos_ref[chunk, :], own_sin_ref[chunk, :]),
            (cos_ref[chunk, :], sin_ref[chunk, :]),
        ]
        size = CHUNK // 2
        select = select_ref[pl.ds(pl.multiple_of(block * size, size), size), :]
        project_chunk(base, phases, fields, weights, select, out_ref, wave_ref)
        return carry

    lax.fori_loop(0, cos_ref.shape[0] // CHUNK, step, 0)


def near_kernel(mine_ref, low_ref, out_ref):
    out_ref[0] = mine_ref[0] + low_ref[1]
    out_ref[1] = mine_ref[1] + low_ref[0]


def last_kernel(kinetic_ref, own_ref, near_ref, far_ref, out_ref):
    out_ref[0] = own_ref[...]
    out_ref[1] = kinetic_ref[...] * own_ref[...] + (near_ref[0] + far_ref[...])


def join_kernel(place_ref, mine_ref, other_ref, once_ref, twice_ref):
    core = place_ref[:, 1:2]
    for number, out_ref in enumerate((once_ref, twice_ref)):
        mine, other = mine_ref[number], other_ref[number]
        half = mine.shape[0] // 2
        first = jnp.where(core == 0, mine, other)
        second = jnp.where(core == 0, other, mine)
        parts = [first[:half, :], second[:half, :], first[half:, :], second[half:, :]]
        out_ref[...] = jnp.concatenate(parts, axis=0)


def potential_kernel(parts_ref, own_potential_ref, potential_ref, out_ref):
    summed = jnp.sum(parts_ref[...].astype(f32), axis=0)
    count = potential_ref.shape[0]
    rows = summed.shape[0] // (2 * count)
    half = rows // 2
    low = lax.broadcasted_iota(jnp.int32, (64, 128), 1) < 64
    results = []
    for pair in range(2 * count):
        source = own_potential_ref if pair < count else potential_ref
        blocks = []
        for part in range(2):
            matrices = source[pair % count, part].astype(f32)
            blocks.append(jnp.where(low, matrices, 0.0))
            blocks.append(jnp.where(low, 0.0, matrices))
        weights = jnp.concatenate(blocks, axis=0).astype(bf16)
        high, middle, lowest = three_parts(summed[pair * rows : (pair + 1) * rows, :])
        pieces = jnp.concatenate(
            [high.astype(f32), middle.astype(f32), lowest.astype(f32)], axis=0
        ).astype(bf16)
        product = dot(pieces, weights, NT)
        product = product[2 * rows :, :] + product[rows : 2 * rows, :] + product[:rows, :]
        real, imag = product[:, :128], product[:, 128:]
        results.append(real[:half, :] - imag[half:, :])
        results.append(real[half:, :] + imag[:half, :])
    applied = jnp.concatenate(results, axis=0).astype(bf16)
    out_ref[...] = jnp.broadcast_to(applied[None], out_ref.shape)


def return_kernel(
    applied_ref, own_template_ref, template_ref, own_cos_ref, own_sin_ref, cos_ref, sin_ref,
    select_ref, out_ref, stack_ref,
):
    atoms = cos_ref.shape[0]
    _, rows, waves = out_ref.shape
    half = rows // 2
    weights = [double_weights(own_template_ref[...]), double_weights(template_ref[...])]
    low = lax.broadcasted_iota(jnp.int32, (1, 128), 1) < 64
    zero = jnp.zeros((rows, waves), f32)

    def step(block, carry):
        base = pl.multiple_of(block * CHUNK, CHUNK)
        chunk = pl.ds(base, CHUNK)
        size = CHUNK // 2
        select = select_ref[pl.ds(pl.multiple_of(block * size, size), size), :]
        height = size * rows
        whole = applied_ref[pl.ds(pl.multiple_of(base // 2 * rows, height), height), :]
        whole = whole.astype(f32)
        for pair in range(size):
            applied = whole[pair * rows : (pair + 1) * rows, :]
            chosen = select[pair : pair + 1, :] > 0.5
            two = slice(2 * pair * rows, 2 * (pair + 1) * rows)
            for kind in range(2):
                take_even = low & chosen if kind == 0 else low & ~chosen
                take_odd = ~low & ~chosen if kind == 0 else ~low & chosen
                split = jnp.concatenate(
                    [jnp.where(take_even, applied, 0.0), jnp.where(take_odd, applied, 0.0)], axis=0
                )
                stack_ref[two, kind * 128 : (kind + 1) * 128] = split.astype(bf16)
        sums = []
        for side, (cosines, sines) in enumerate(((own_cos_ref, own_sin_ref), (cos_ref, sin_ref))):
            straight, turned = carry[side]
            cosine, sine = cosines[chunk, :], sines[chunk, :]
            images = dot(stack_ref[...], weights[side], NN)
            for atom in range(CHUNK):
                image = images[atom * rows : (atom + 1) * rows, :]
                straight = straight + cosine[atom : atom + 1, :] * image
                turned = turned + sine[atom : atom + 1, :] * image
            sums.append((straight, turned))
        return tuple(sums)

    sums = lax.fori_loop(0, atoms // CHUNK, step, ((zero, zero), (zero, zero)))
    for side, (straight, turned) in enumerate(sums):
        real = straight[:half, :] + turned[half:, :]
        imag = straight[half:, :] - turned[:half, :]
        out_ref[side] = jnp.concatenate([real, imag], axis=0)


def vmem(count):
    return [pl.BlockSpec(memory_space=pltpu.VMEM)] * count


def shape(dims, dtype):
    return jax.ShapeDtypeStruct(dims, dtype)


def call(kernel, args, out_shape, name, scratch_shapes=(), unread=0):
    return pl.pallas_call(
        kernel,
        in_specs=vmem(len(args) - unread) + [pl.BlockSpec(memory_space=pltpu.HBM)] * unread,
        out_specs=tuple(vmem(len(out_shape))),
        out_shape=tuple(out_shape),
        scratch_shapes=scratch_shapes,
        compiler_params=LIMIT,
        name=name,
    )(*args)


def flip(array, *axes):
    pairs = [(place, 2 ** len(axes) - 1 - place) for place in range(2 ** len(axes))]
    return lax.ppermute(array, axes, pairs)


def per_device(bands_in, template, potential, miller, positions, species, atom_order, reciprocal):
    plane = lax.axis_size("zx")
    groups = lax.axis_size("yh") * lax.axis_size("core")
    slot_dev = potential.shape[0]
    atoms = 2 * slot_dev * plane
    species_count, harmonics, waves = template.shape
    bands = bands_in.shape[1]
    rows = bands
    pairs = slot_dev // 2
    message = 2 * pairs * rows
    width = 2 * harmonics
    template = template.reshape(species_count * harmonics, waves)
    fields = bands_in.reshape(2 * bands, waves)
    core = lax.axis_index("core")
    stride = groups * slot_dev
    first_slot = lax.axis_index("yl") * plane * stride + lax.axis_index("yh") * 2 * slot_dev
    place = jnp.stack([first_slot, core]).astype(jnp.int32).reshape(1, 2)
    lengths = reciprocal.reshape(1, 3)
    coefs_shape = shape((atoms // 2 * rows, width), bf16)
    fields_shape = shape((rows, waves), f32)
    whole_shape = shape((2 * bands, waves), f32)
    phase_shape = shape((atoms, waves), f32)
    kinetic_shape = shape((1, waves), f32)
    weights_shape = shape((2 * width, waves), bf16)
    wave_scratch = pltpu.VMEM((2, CHUNK * rows, waves), bf16)

    other_miller = flip(miller, "yl")
    other_fields = flip(fields, "yl")
    other_template = flip(template, "yl")

    def matrices_of(potential):
        matrices = potential.reshape(pairs, 2, 2, harmonics, harmonics)
        return matrices.transpose(0, 2, 3, 1, 4).reshape(pairs, 2, harmonics, width)

    matrices, other_matrices = matrices_of(potential), matrices_of(flip(potential, "core"))
    inputs = (
        atom_order.reshape(1, -1), positions, species.reshape(1, -1), miller, lengths, fields,
        template,
    )
    inputs = tuple(pltpu.with_memory_space_constraint(value, pltpu.HBM) for value in inputs)
    own_cos, own_sin, select, table, own, own_kinetic, own_both, lengths = call(
        functools.partial(prepare_kernel, stride, slot_dev),
        (place,) + inputs,
        (
            phase_shape, phase_shape, shape((atoms // 2, 128), f32), shape((atoms, 16), f32),
            fields_shape, kinetic_shape, weights_shape, shape(lengths.shape, f32),
        ),
        "prepare",
        [pltpu.VMEM(value.shape, value.dtype) for value in inputs]
        + [pltpu.SemaphoreType.DMA((len(inputs),))],
        unread=len(inputs),
    )
    coefs, other_cos, other_sin, other, other_kinetic, other_both = call(
        first_kernel,
        (
            place, lengths, table, other_miller, own, other_fields, own_both, other_template,
            own_cos, own_sin, select, matrices, other_matrices,
        ),
        (
            coefs_shape, phase_shape, phase_shape, fields_shape, kinetic_shape, weights_shape,
        ),
        "first",
        [wave_scratch],
    )
    phases = (own_cos, own_sin, other_cos, other_sin, select)

    def return_fields(coefs):
        parts = lax.all_to_all(coefs.reshape(plane, message, width), "zx", 0, 0, tiled=True)
        (applied,) = call(
            potential_kernel,
            (parts, matrices, other_matrices),
            (shape((plane, message, width), bf16),),
            "potential",
        )
        applied = lax.all_to_all(applied, "zx", 0, 0, tiled=True)
        (mine,) = call(
            return_kernel,
            (applied.reshape(atoms // 2 * rows, width), template, other_template) + phases,
            (shape((2, rows, waves), f32),),
            "back",
            [pltpu.VMEM((CHUNK * rows, 2 * width), bf16)],
        )
        (near,) = call(
            near_kernel, (mine, flip(mine, "yl")), (shape((2, rows, waves), f32),), "near"
        )
        return near

    near = return_fields(coefs)
    once, coefs = call(
        next_kernel,
        (
            own_kinetic, other_kinetic, own, other, near, flip(near, "yl", "yh"), own_both,
            other_both,
        )
        + phases,
        (fields_shape, coefs_shape),
        "next",
        [wave_scratch],
    )
    near = return_fields(coefs)
    (mine,) = call(
        last_kernel,
        (own_kinetic, once, near, flip(near[1], "yl", "yh")),
        (shape((2, rows, waves), f32),),
        "last",
    )
    once, twice = call(
        join_kernel, (place, mine, flip(mine, "core")), (whole_shape, whole_shape), "join"
    )
    return once.reshape(bands_in.shape), twice.reshape(bands_in.shape)


def solution(mesh):
    pw, groups = mesh.devices.shape
    fine = Mesh(mesh.devices.reshape(2, pw // 2, 2, groups // 2), ("yl", "zx", "yh", "core"))
    waves, slots = ("yl", "zx"), ("yl", "zx", "yh", "core")
    in_specs = (
        P(None, None, waves),
        P(None, None, waves),
        P(slots, None),
        P(None, waves),
        P(),
        P(),
        P(),
        P(),
    )
    out_specs = (P(None, None, waves), P(None, None, waves))
    return jax.shard_map(
        per_device, mesh=fine, in_specs=in_specs, out_specs=out_specs, check_vma=False
    )
```

```python
import functools

import jax
import jax.numpy as jnp
from jax import lax
from jax.experimental import pallas as pl
from jax.experimental.pallas import tpu as pltpu
from jax.sharding import Mesh
from jax.sharding import PartitionSpec as P


f32 = jnp.float32
bf16 = jnp.bfloat16

COS_TURN = (
    0.9999992107823212,
    -19.738980355764024,
    64.92865742103461,
    -85.27162153431523,
    58.790492120199225,
    -21.07110562773966,
)
SIN_TURN = (
    6.283184916495427,
    -41.34158923268859,
    81.59994332978516,
    -76.61447253128296,
    41.342882354732154,
    -12.471243535293539,
)
NT = (((1,), (1,)), ((), ()))
NN = (((1,), (0,)), ((), ()))
CHUNK = 128
STEP = 256
LIMIT = pltpu.CompilerParams(vmem_limit_bytes=12 * 2**20)


def dot(left, right, dims):
    return lax.dot_general(left, right, dims, preferred_element_type=f32)


def horner(coefs, arg):
    total = jnp.full_like(arg, coefs[-1])
    for coef in coefs[-2::-1]:
        total = total * arg + coef
    return total


def three_parts(values):
    high = values.astype(bf16)
    rest = values - high.astype(f32)
    middle = rest.astype(bf16)
    low = (rest - middle.astype(f32)).astype(bf16)
    return high, middle, low


def atom_table(positions, species, order, first_slot, core, rows, stride, slot_dev):
    atoms = order.shape[1]
    row = lax.broadcasted_iota(jnp.int32, (rows, 1), 0)
    pair = 2 * slot_dev
    side = (row % pair // slot_dev) ^ core
    slot = first_slot + row // pair * stride + side * slot_dev + row % slot_dev
    lane = lax.broadcasted_iota(jnp.int32, (rows, atoms), 1)
    pick_slot = jnp.where(lane == slot, 1.0, 0.0).astype(bf16)
    coarse, fine = order // 128, order % 128
    pad = jnp.zeros((14, atoms), f32)
    digits = jnp.concatenate([coarse.astype(f32), fine.astype(f32), pad], axis=0).astype(bf16)
    found = dot(pick_slot, digits, NT)
    atom = (found[:, 0:1] * 128.0 + found[:, 1:2]).astype(jnp.int32)
    pick_atom = jnp.where(lane == atom, 1.0, 0.0).astype(bf16)
    high, middle, low = three_parts(positions)
    pad = jnp.zeros((6, atoms), bf16)
    facts = jnp.concatenate([high, middle, low, species.astype(f32).astype(bf16), pad], axis=0)
    return dot(pick_atom, facts, NT)


def field_pair(fields):
    half = fields.shape[0] // 2
    return fields, jnp.concatenate([-fields[half:, :], fields[:half, :]], axis=0)


def core_bands(fields_ref, core):
    quarter = fields_ref.shape[0] // 4
    parts = [fields_ref[part * quarter : (part + 1) * quarter, :] for part in range(4)]
    first = jnp.concatenate([parts[0], parts[2]], axis=0)
    second = jnp.concatenate([parts[1], parts[3]], axis=0)
    return jnp.where(core == 0, first, second)


def phases_of(table, miller):
    turns = jnp.zeros((table.shape[0], miller.shape[1]), f32)
    for axis in range(3):
        centre = table[:, axis : axis + 1] + table[:, 3 + axis : 4 + axis]
        centre = centre + table[:, 6 + axis : 7 + axis]
        turns = turns + centre * miller[axis : axis + 1, :]
    turns = turns - jnp.round(turns)
    square = turns * turns
    return horner(COS_TURN, square), turns * horner(SIN_TURN, square)


def kinetic_of(miller, lengths):
    total = jnp.zeros((1, miller.shape[1]), f32)
    for axis in range(3):
        wave_number = lengths[:, axis : axis + 1] * miller[axis : axis + 1, :]
        total = total + wave_number * wave_number
    return 0.5 * total


def both_weights(template):
    low, high = template[:64, :], template[64:, :]
    return jnp.concatenate([low, high, high, low], axis=0)


def double_weights(template):
    low, high = template[:64, :], template[64:, :]
    return jnp.concatenate([low, low, high, high], axis=0)


def prepare_kernel(
    stride, slot_dev, place_ref, *refs,
):
    sources, refs = refs[:7], refs[7:]
    cos_ref, sin_ref, select_ref, table_ref, own_ref, kinetic_ref, both_ref, kept_ref = refs[:8]
    targets, semaphores = refs[8:15], refs[15]
    copies = [
        pltpu.make_async_copy(source, target, semaphores.at[number])
        for number, (source, target) in enumerate(zip(sources, targets))
    ]
    for copy in copies:
        copy.start()
    for copy in copies[:5]:
        copy.wait()
    order_ref, positions_ref, species_ref, miller_ref = targets[:4]
    lengths_ref, fields_ref, template_ref = targets[4:]
    kept_ref[...] = lengths_ref[...]
    atoms = cos_ref.shape[0]
    core = place_ref[:, 1:2]
    table_ref[...] = atom_table(
        positions_ref[...], species_ref[...], order_ref[...], place_ref[:, 0:1], core, atoms,
        stride, slot_dev,
    )
    miller = miller_ref[...].astype(f32)
    kinetic_ref[...] = kinetic_of(miller, lengths_ref[...])
    low = lax.broadcasted_iota(jnp.int32, (1, 128), 1) < 64

    def step(block, carry):
        base = pl.multiple_of(block * STEP, STEP)
        table = table_ref[pl.ds(base, STEP), :]
        cosine, sine = phases_of(table, miller)
        cos_ref[pl.ds(base, STEP), :] = cosine
        sin_ref[pl.ds(base, STEP), :] = sine
        kinds = table[:, 9:10]
        picked = []
        for pair in range(STEP // 2):
            even = 1.0 - kinds[2 * pair : 2 * pair + 1, :]
            odd = kinds[2 * pair + 1 : 2 * pair + 2, :]
            picked.append(jnp.where(low, even, odd))
        half = pl.ds(pl.multiple_of(block * (STEP // 2), STEP // 2), STEP // 2)
        select_ref[half, :] = jnp.concatenate(picked, axis=0)
        return carry

    lax.fori_loop(0, atoms // STEP, step, 0)
    for copy in copies[5:]:
        copy.wait()
    own_ref[...] = core_bands(fields_ref, core)
    both_ref[...] = both_weights(template_ref[...])


def project_chunk(base, phases, fields, weights, select, out_ref, wave_ref):
    rows = fields[0][0].shape[0]
    products = []
    for side in range(2):
        cosine, sine = phases[side]
        straight, turned = fields[side]
        for pair in range(CHUNK // 2):
            waves = [
                cosine[atom : atom + 1, :] * straight + sine[atom : atom + 1, :] * turned
                for atom in (2 * pair, 2 * pair + 1)
            ]
            two = slice(2 * pair * rows, 2 * (pair + 1) * rows)
            wave_ref[side, two, :] = jnp.concatenate(waves, axis=0).astype(bf16)
        products.append(dot(wave_ref[side], weights[side][...], NT))
    both = products[0] + products[1]
    low = lax.broadcasted_iota(jnp.int32, (rows, 128), 1) < 64
    results = []
    for pair in range(CHUNK // 2):
        even = both[2 * pair * rows : (2 * pair + 1) * rows, :]
        odd = both[(2 * pair + 1) * rows : (2 * pair + 2) * rows, :]
        first = jnp.where(low, even[:, :128], odd[:, :128])
        second = jnp.where(low, even[:, 128:], odd[:, 128:])
        results.append(jnp.where(select[pair : pair + 1, :] > 0.5, first, second))
    size = CHUNK // 2 * rows
    start = pl.multiple_of(base // 2 * rows, size)
    out_ref[pl.ds(start, size), :] = jnp.concatenate(results, axis=0).astype(bf16)


def first_kernel(
    place_ref, lengths_ref, table_ref, miller_ref, own_ref, fields_ref, own_both_ref,
    template_ref, own_cos_ref, own_sin_ref, select_ref, out_ref, cos_ref, sin_ref, other_ref,
    kinetic_ref, both_ref, wave_ref,
):
    miller = miller_ref[...].astype(f32)
    kinetic_ref[...] = kinetic_of(miller, lengths_ref[...])
    other = core_bands(fields_ref, place_ref[:, 1:2])
    other_ref[...] = other
    fields = [field_pair(own_ref[...]), field_pair(other)]
    both_ref[...] = both_weights(template_ref[...])
    weights = [own_both_ref, both_ref]

    def step(block, carry):
        base = pl.multiple_of(block * CHUNK, CHUNK)
        chunk = pl.ds(base, CHUNK)
        cosine, sine = phases_of(table_ref[chunk, :], miller)
        cos_ref[chunk, :] = cosine
        sin_ref[chunk, :] = sine
        phases = [(own_cos_ref[chunk, :], own_sin_ref[chunk, :]), (cosine, sine)]
        size = CHUNK // 2
        select = select_ref[pl.ds(pl.multiple_of(block * size, size), size), :]
        project_chunk(base, phases, fields, weights, select, out_ref, wave_ref)
        return carry

    lax.fori_loop(0, cos_ref.shape[0] // CHUNK, step, 0)


def next_kernel(
    own_kinetic_ref, kinetic_ref, own_ref, other_ref, mine_ref, low_ref, high_ref,
    both_ref, own_weights_ref, weights_ref, own_cos_ref, own_sin_ref, cos_ref, sin_ref, select_ref,
    fields_out_ref, out_ref, wave_ref,
):
    own = own_kinetic_ref[...] * own_ref[...]
    own = own + ((mine_ref[0] + high_ref[0]) + (low_ref[1] + both_ref[1]))
    fields_out_ref[...] = own
    other = kinetic_ref[...] * other_ref[...]
    other = other + ((mine_ref[1] + high_ref[1]) + (low_ref[0] + both_ref[0]))
    fields = [field_pair(own), field_pair(other)]
    weights = [own_weights_ref, weights_ref]

    def step(block, carry):
        base = pl.multiple_of(block * CHUNK, CHUNK)
        chunk = pl.ds(base, CHUNK)
        phases = [
            (own_cos_ref[chunk, :], own_sin_ref[chunk, :]),
            (cos_ref[chunk, :], sin_ref[chunk, :]),
        ]
        size = CHUNK // 2
        select = select_ref[pl.ds(pl.multiple_of(block * size, size), size), :]
        project_chunk(base, phases, fields, weights, select, out_ref, wave_ref)
        return carry

    lax.fori_loop(0, cos_ref.shape[0] // CHUNK, step, 0)


def last_kernel(kinetic_ref, own_ref, mine_ref, low_ref, high_ref, both_ref, out_ref):
    total = kinetic_ref[...] * own_ref[...]
    out_ref[0] = own_ref[...]
    out_ref[1] = total + ((mine_ref[0] + high_ref[...]) + (low_ref[...] + both_ref[...]))


def join_kernel(place_ref, mine_ref, other_ref, once_ref, twice_ref):
    core = place_ref[:, 1:2]
    for number, out_ref in enumerate((once_ref, twice_ref)):
        mine, other = mine_ref[number], other_ref[number]
        half = mine.shape[0] // 2
        first = jnp.where(core == 0, mine, other)
        second = jnp.where(core == 0, other, mine)
        parts = [first[:half, :], second[:half, :], first[half:, :], second[half:, :]]
        out_ref[...] = jnp.concatenate(parts, axis=0)


def potential_kernel(parts_ref, own_potential_ref, potential_ref, out_ref):
    summed = jnp.sum(parts_ref[...].astype(f32), axis=0)
    count = potential_ref.shape[0]
    rows = summed.shape[0] // (2 * count)
    half = rows // 2
    low = lax.broadcasted_iota(jnp.int32, (64, 128), 1) < 64
    results = []
    for pair in range(2 * count):
        source = own_potential_ref if pair < count else potential_ref
        blocks = []
        for part in range(2):
            matrices = source[pair % count, part].astype(f32)
            blocks.append(jnp.where(low, matrices, 0.0))
            blocks.append(jnp.where(low, 0.0, matrices))
        weights = jnp.concatenate(blocks, axis=0).astype(bf16)
        high, middle, lowest = three_parts(summed[pair * rows : (pair + 1) * rows, :])
        pieces = jnp.concatenate(
            [high.astype(f32), middle.astype(f32), lowest.astype(f32)], axis=0
        ).astype(bf16)
        product = dot(pieces, weights, NT)
        product = product[2 * rows :, :] + product[rows : 2 * rows, :] + product[:rows, :]
        real, imag = product[:, :128], product[:, 128:]
        results.append(real[:half, :] - imag[half:, :])
        results.append(real[half:, :] + imag[:half, :])
    applied = jnp.concatenate(results, axis=0).astype(bf16)
    out_ref[...] = jnp.broadcast_to(applied[None], out_ref.shape)


def return_kernel(
    applied_ref, own_template_ref, template_ref, own_cos_ref, own_sin_ref, cos_ref, sin_ref,
    select_ref, out_ref, stack_ref,
):
    atoms = cos_ref.shape[0]
    _, rows, waves = out_ref.shape
    half = rows // 2
    weights = [double_weights(own_template_ref[...]), double_weights(template_ref[...])]
    low = lax.broadcasted_iota(jnp.int32, (1, 128), 1) < 64
    zero = jnp.zeros((rows, waves), f32)

    def step(block, carry):
        base = pl.multiple_of(block * CHUNK, CHUNK)
        chunk = pl.ds(base, CHUNK)
        size = CHUNK // 2
        select = select_ref[pl.ds(pl.multiple_of(block * size, size), size), :]
        height = size * rows
        whole = applied_ref[pl.ds(pl.multiple_of(base // 2 * rows, height), height), :]
        whole = whole.astype(f32)
        for pair in range(size):
            applied = whole[pair * rows : (pair + 1) * rows, :]
            chosen = select[pair : pair + 1, :] > 0.5
            two = slice(2 * pair * rows, 2 * (pair + 1) * rows)
            for kind in range(2):
                take_even = low & chosen if kind == 0 else low & ~chosen
                take_odd = ~low & ~chosen if kind == 0 else ~low & chosen
                split = jnp.concatenate(
                    [jnp.where(take_even, applied, 0.0), jnp.where(take_odd, applied, 0.0)], axis=0
                )
                stack_ref[two, kind * 128 : (kind + 1) * 128] = split.astype(bf16)
        sums = []
        for side, (cosines, sines) in enumerate(((own_cos_ref, own_sin_ref), (cos_ref, sin_ref))):
            straight, turned = carry[side]
            cosine, sine = cosines[chunk, :], sines[chunk, :]
            images = dot(stack_ref[...], weights[side], NN)
            for atom in range(CHUNK):
                image = images[atom * rows : (atom + 1) * rows, :]
                straight = straight + cosine[atom : atom + 1, :] * image
                turned = turned + sine[atom : atom + 1, :] * image
            sums.append((straight, turned))
        return tuple(sums)

    sums = lax.fori_loop(0, atoms // CHUNK, step, ((zero, zero), (zero, zero)))
    for side, (straight, turned) in enumerate(sums):
        real = straight[:half, :] + turned[half:, :]
        imag = straight[half:, :] - turned[:half, :]
        out_ref[side] = jnp.concatenate([real, imag], axis=0)


def vmem(count):
    return [pl.BlockSpec(memory_space=pltpu.VMEM)] * count


def shape(dims, dtype):
    return jax.ShapeDtypeStruct(dims, dtype)


def call(kernel, args, out_shape, scratch_shapes=(), unread=0):
    return pl.pallas_call(
        kernel,
        in_specs=vmem(len(args) - unread) + [pl.BlockSpec(memory_space=pltpu.HBM)] * unread,
        out_specs=tuple(vmem(len(out_shape))),
        out_shape=tuple(out_shape),
        scratch_shapes=scratch_shapes,
        compiler_params=LIMIT,
    )(*args)


def flip(array, *axes):
    pairs = [(place, 2 ** len(axes) - 1 - place) for place in range(2 ** len(axes))]
    return lax.ppermute(array, axes, pairs)


def per_device(bands_in, template, potential, miller, positions, species, atom_order, reciprocal):
    plane = lax.axis_size("zx")
    groups = lax.axis_size("yh") * lax.axis_size("core")
    slot_dev = potential.shape[0]
    atoms = 2 * slot_dev * plane
    species_count, harmonics, waves = template.shape
    bands = bands_in.shape[1]
    rows = bands
    pairs = slot_dev // 2
    message = 2 * pairs * rows
    width = 2 * harmonics
    template = template.reshape(species_count * harmonics, waves)
    fields = bands_in.reshape(2 * bands, waves)
    matrices = potential.reshape(pairs, 2, 2, harmonics, harmonics)
    matrices = matrices.transpose(0, 2, 3, 1, 4).reshape(pairs, 2, harmonics, width)
    core = lax.axis_index("core")
    stride = groups * slot_dev
    first_slot = lax.axis_index("yl") * plane * stride + lax.axis_index("yh") * 2 * slot_dev
    place = jnp.stack([first_slot, core]).astype(jnp.int32).reshape(1, 2)
    lengths = reciprocal.reshape(1, 3)
    coefs_shape = shape((atoms // 2 * rows, width), bf16)
    fields_shape = shape((rows, waves), f32)
    whole_shape = shape((2 * bands, waves), f32)
    phase_shape = shape((atoms, waves), f32)
    kinetic_shape = shape((1, waves), f32)
    weights_shape = shape((2 * width, waves), bf16)
    wave_scratch = pltpu.VMEM((2, CHUNK * rows, waves), bf16)

    other_miller = flip(miller, "yl")
    other_fields = flip(fields, "yl")
    other_template = flip(template, "yl")
    inputs = (
        atom_order.reshape(1, -1), positions, species.reshape(1, -1), miller, lengths, fields,
        template,
    )
    inputs = tuple(pltpu.with_memory_space_constraint(value, pltpu.HBM) for value in inputs)
    own_cos, own_sin, select, table, own, own_kinetic, own_both, lengths = call(
        functools.partial(prepare_kernel, stride, slot_dev),
        (place,) + inputs,
        (
            phase_shape, phase_shape, shape((atoms // 2, 128), f32), shape((atoms, 16), f32),
            fields_shape, kinetic_shape, weights_shape, shape(lengths.shape, f32),
        ),
        [pltpu.VMEM(value.shape, value.dtype) for value in inputs]
        + [pltpu.SemaphoreType.DMA((len(inputs),))],
        unread=len(inputs),
    )
    coefs, other_cos, other_sin, other, other_kinetic, other_both = call(
        first_kernel,
        (
            place, lengths, table, other_miller, own, other_fields, own_both, other_template,
            own_cos, own_sin, select,
        ),
        (
            coefs_shape, phase_shape, phase_shape, fields_shape, kinetic_shape, weights_shape,
        ),
        [wave_scratch],
    )
    other_matrices = flip(matrices, "core")
    phases = (own_cos, own_sin, other_cos, other_sin, select)

    def return_fields(coefs):
        parts = lax.all_to_all(coefs.reshape(plane, message, width), "zx", 0, 0, tiled=True)
        (applied,) = call(
            potential_kernel,
            (parts, matrices, other_matrices),
            (shape((plane, message, width), bf16),),
        )
        applied = lax.all_to_all(applied, "zx", 0, 0, tiled=True)
        (mine,) = call(
            return_kernel,
            (applied.reshape(atoms // 2 * rows, width), template, other_template) + phases,
            (shape((2, rows, waves), f32),),
            [pltpu.VMEM((CHUNK * rows, 2 * width), bf16)],
        )
        return mine

    def around(same, turned):
        low = flip(turned, "yl")
        both = flip(turned, "yl", "yh")
        high = flip(same, "yh")
        return low, high, both

    mine = return_fields(coefs)
    once, coefs = call(
        next_kernel,
        (own_kinetic, other_kinetic, own, other, mine)
        + around(mine, mine)
        + (own_both, other_both)
        + phases,
        (fields_shape, coefs_shape),
        [wave_scratch],
    )
    mine = return_fields(coefs)
    (mine,) = call(
        last_kernel,
        (own_kinetic, once, mine) + around(mine[0], mine[1]),
        (shape((2, rows, waves), f32),),
    )
    once, twice = call(join_kernel, (place, mine, flip(mine, "core")), (whole_shape, whole_shape))
    return once.reshape(bands_in.shape), twice.reshape(bands_in.shape)


def solution(mesh):
    pw, groups = mesh.devices.shape
    fine = Mesh(mesh.devices.reshape(2, pw // 2, 2, groups // 2), ("yl", "zx", "yh", "core"))
    waves, slots = ("yl", "zx"), ("yl", "zx", "yh", "core")
    in_specs = (
        P(None, None, waves),
        P(None, None, waves),
        P(slots, None),
        P(None, waves),
        P(),
        P(),
        P(),
        P(),
    )
    out_specs = (P(None, None, waves), P(None, None, waves))

    return jax.shard_map(
        per_device, mesh=fine, in_specs=in_specs, out_specs=out_specs, check_vma=False
    )
```

```python
import functools

import jax
import jax.numpy as jnp
from jax import lax
from jax.experimental import pallas as pl
from jax.experimental.pallas import tpu as pltpu
from jax.sharding import Mesh
from jax.sharding import PartitionSpec as P


f32 = jnp.float32
bf16 = jnp.bfloat16

COS_TURN = (
    0.9999992107823212,
    -19.738980355764024,
    64.92865742103461,
    -85.27162153431523,
    58.790492120199225,
    -21.07110562773966,
)
SIN_TURN = (
    6.283184916495427,
    -41.34158923268859,
    81.59994332978516,
    -76.61447253128296,
    41.342882354732154,
    -12.471243535293539,
)
NT = (((1,), (1,)), ((), ()))
NN = (((1,), (0,)), ((), ()))
CHUNK = 128
STEP = 256
LIMIT = pltpu.CompilerParams(vmem_limit_bytes=12 * 2**20)


def dot(left, right, dims):
    return lax.dot_general(left, right, dims, preferred_element_type=f32)


def horner(coefs, arg):
    total = jnp.full_like(arg, coefs[-1])
    for coef in coefs[-2::-1]:
        total = total * arg + coef
    return total


def three_parts(values):
    high = values.astype(bf16)
    rest = values - high.astype(f32)
    middle = rest.astype(bf16)
    low = (rest - middle.astype(f32)).astype(bf16)
    return high, middle, low


def atom_table(positions, species, order, first_slot, core, rows, stride, slot_dev):
    atoms = order.shape[1]
    row = lax.broadcasted_iota(jnp.int32, (rows, 1), 0)
    pair = 2 * slot_dev
    side = (row % pair // slot_dev) ^ core
    member = row // pair
    member = member % 8 * (rows // pair // 8) + member // 8
    slot = first_slot + member * stride + side * slot_dev + row % slot_dev
    lane = lax.broadcasted_iota(jnp.int32, (rows, atoms), 1)
    pick_slot = jnp.where(lane == slot, 1.0, 0.0).astype(bf16)
    coarse, fine = order // 128, order % 128
    pad = jnp.zeros((14, atoms), f32)
    digits = jnp.concatenate([coarse.astype(f32), fine.astype(f32), pad], axis=0).astype(bf16)
    found = dot(pick_slot, digits, NT)
    atom = (found[:, 0:1] * 128.0 + found[:, 1:2]).astype(jnp.int32)
    pick_atom = jnp.where(lane == atom, 1.0, 0.0).astype(bf16)
    high, middle, low = three_parts(positions)
    pad = jnp.zeros((6, atoms), bf16)
    facts = jnp.concatenate([high, middle, low, species.astype(f32).astype(bf16), pad], axis=0)
    return dot(pick_atom, facts, NT)


def field_pair(fields):
    half = fields.shape[0] // 2
    return fields, jnp.concatenate([-fields[half:, :], fields[:half, :]], axis=0)


def core_bands(fields_ref, core):
    quarter = fields_ref.shape[0] // 4
    parts = [fields_ref[part * quarter : (part + 1) * quarter, :] for part in range(4)]
    first = jnp.concatenate([parts[0], parts[2]], axis=0)
    second = jnp.concatenate([parts[1], parts[3]], axis=0)
    return jnp.where(core == 0, first, second)


def phases_of(table, miller):
    turns = jnp.zeros((table.shape[0], miller.shape[1]), f32)
    for axis in range(3):
        centre = table[:, axis : axis + 1] + table[:, 3 + axis : 4 + axis]
        centre = centre + table[:, 6 + axis : 7 + axis]
        turns = turns + centre * miller[axis : axis + 1, :]
    turns = turns - jnp.round(turns)
    square = turns * turns
    return horner(COS_TURN, square), turns * horner(SIN_TURN, square)


def kinetic_of(miller, lengths):
    total = jnp.zeros((1, miller.shape[1]), f32)
    for axis in range(3):
        wave_number = lengths[:, axis : axis + 1] * miller[axis : axis + 1, :]
        total = total + wave_number * wave_number
    return 0.5 * total


def both_weights(template):
    low, high = template[:64, :], template[64:, :]
    return jnp.concatenate([low, high, high, low], axis=0)


def double_weights(template):
    low, high = template[:64, :], template[64:, :]
    return jnp.concatenate([low, low, high, high], axis=0)


def prepare_kernel(
    stride, slot_dev, place_ref, *refs,
):
    sources, refs = refs[:7], refs[7:]
    cos_ref, sin_ref, select_ref, table_ref, own_ref, kinetic_ref, both_ref, kept_ref = refs[:8]
    targets, semaphores = refs[8:15], refs[15]
    copies = [
        pltpu.make_async_copy(source, target, semaphores.at[number])
        for number, (source, target) in enumerate(zip(sources, targets))
    ]
    for copy in copies:
        copy.start()
    for copy in copies[:5]:
        copy.wait()
    order_ref, positions_ref, species_ref, miller_ref = targets[:4]
    lengths_ref, fields_ref, template_ref = targets[4:]
    kept_ref[...] = lengths_ref[...]
    atoms = cos_ref.shape[0]
    core = place_ref[:, 1:2]
    table_ref[...] = atom_table(
        positions_ref[...], species_ref[...], order_ref[...], place_ref[:, 0:1], core, atoms,
        stride, slot_dev,
    )
    miller = miller_ref[...].astype(f32)
    kinetic_ref[...] = kinetic_of(miller, lengths_ref[...])
    low = lax.broadcasted_iota(jnp.int32, (1, 128), 1) < 64

    def step(block, carry):
        base = pl.multiple_of(block * STEP, STEP)
        table = table_ref[pl.ds(base, STEP), :]
        cosine, sine = phases_of(table, miller)
        cos_ref[pl.ds(base, STEP), :] = cosine
        sin_ref[pl.ds(base, STEP), :] = sine
        kinds = table[:, 9:10]
        picked = []
        for pair in range(STEP // 2):
            even = 1.0 - kinds[2 * pair : 2 * pair + 1, :]
            odd = kinds[2 * pair + 1 : 2 * pair + 2, :]
            picked.append(jnp.where(low, even, odd))
        half = pl.ds(pl.multiple_of(block * (STEP // 2), STEP // 2), STEP // 2)
        select_ref[half, :] = jnp.concatenate(picked, axis=0)
        return carry

    lax.fori_loop(0, atoms // STEP, step, 0)
    for copy in copies[5:]:
        copy.wait()
    own_ref[...] = core_bands(fields_ref, core)
    both_ref[...] = both_weights(template_ref[...])


def project_chunk(base, phases, fields, weights, select, out_ref, wave_ref):
    rows = fields[0][0].shape[0]
    products = []
    for side in range(2):
        cosine, sine = phases[side]
        straight, turned = fields[side]
        for pair in range(CHUNK // 2):
            waves = [
                cosine[atom : atom + 1, :] * straight + sine[atom : atom + 1, :] * turned
                for atom in (2 * pair, 2 * pair + 1)
            ]
            two = slice(2 * pair * rows, 2 * (pair + 1) * rows)
            wave_ref[side, two, :] = jnp.concatenate(waves, axis=0).astype(bf16)
        products.append(dot(wave_ref[side], weights[side][...], NT))
    both = products[0] + products[1]
    low = lax.broadcasted_iota(jnp.int32, (rows, 128), 1) < 64
    results = []
    for pair in range(CHUNK // 2):
        even = both[2 * pair * rows : (2 * pair + 1) * rows, :]
        odd = both[(2 * pair + 1) * rows : (2 * pair + 2) * rows, :]
        first = jnp.where(low, even[:, :128], odd[:, :128])
        second = jnp.where(low, even[:, 128:], odd[:, 128:])
        results.append(jnp.where(select[pair : pair + 1, :] > 0.5, first, second))
    size = CHUNK // 2 * rows
    start = pl.multiple_of(base // 2 * rows, size)
    out_ref[pl.ds(start, size), :] = jnp.concatenate(results, axis=0).astype(bf16)


def first_kernel(
    place_ref, lengths_ref, table_ref, miller_ref, own_ref, fields_ref, own_both_ref,
    template_ref, own_cos_ref, own_sin_ref, select_ref, out_ref, cos_ref, sin_ref, other_ref,
    kinetic_ref, both_ref, wave_ref,
):
    miller = miller_ref[...].astype(f32)
    kinetic_ref[...] = kinetic_of(miller, lengths_ref[...])
    other = core_bands(fields_ref, place_ref[:, 1:2])
    other_ref[...] = other
    fields = [field_pair(own_ref[...]), field_pair(other)]
    both_ref[...] = both_weights(template_ref[...])
    weights = [own_both_ref, both_ref]

    def step(block, carry):
        base = pl.multiple_of(block * CHUNK, CHUNK)
        chunk = pl.ds(base, CHUNK)
        cosine, sine = phases_of(table_ref[chunk, :], miller)
        cos_ref[chunk, :] = cosine
        sin_ref[chunk, :] = sine
        phases = [(own_cos_ref[chunk, :], own_sin_ref[chunk, :]), (cosine, sine)]
        size = CHUNK // 2
        select = select_ref[pl.ds(pl.multiple_of(block * size, size), size), :]
        project_chunk(base, phases, fields, weights, select, out_ref, wave_ref)
        return carry

    lax.fori_loop(0, cos_ref.shape[0] // CHUNK, step, 0)


def next_kernel(
    own_kinetic_ref, kinetic_ref, own_ref, other_ref, mine_ref, low_ref, high_ref,
    both_ref, own_weights_ref, weights_ref, own_cos_ref, own_sin_ref, cos_ref, sin_ref, select_ref,
    fields_out_ref, out_ref, wave_ref,
):
    own = own_kinetic_ref[...] * own_ref[...]
    own = own + ((mine_ref[0] + high_ref[0]) + (low_ref[1] + both_ref[1]))
    fields_out_ref[...] = own
    other = kinetic_ref[...] * other_ref[...]
    other = other + ((mine_ref[1] + high_ref[1]) + (low_ref[0] + both_ref[0]))
    fields = [field_pair(own), field_pair(other)]
    weights = [own_weights_ref, weights_ref]

    def step(block, carry):
        base = pl.multiple_of(block * CHUNK, CHUNK)
        chunk = pl.ds(base, CHUNK)
        phases = [
            (own_cos_ref[chunk, :], own_sin_ref[chunk, :]),
            (cos_ref[chunk, :], sin_ref[chunk, :]),
        ]
        size = CHUNK // 2
        select = select_ref[pl.ds(pl.multiple_of(block * size, size), size), :]
        project_chunk(base, phases, fields, weights, select, out_ref, wave_ref)
        return carry

    lax.fori_loop(0, cos_ref.shape[0] // CHUNK, step, 0)


def last_kernel(kinetic_ref, own_ref, mine_ref, low_ref, high_ref, both_ref, out_ref):
    total = kinetic_ref[...] * own_ref[...]
    out_ref[0] = own_ref[...]
    out_ref[1] = total + ((mine_ref[0] + high_ref[...]) + (low_ref[...] + both_ref[...]))


def join_kernel(place_ref, mine_ref, other_ref, once_ref, twice_ref):
    core = place_ref[:, 1:2]
    for number, out_ref in enumerate((once_ref, twice_ref)):
        mine, other = mine_ref[number], other_ref[number]
        half = mine.shape[0] // 2
        first = jnp.where(core == 0, mine, other)
        second = jnp.where(core == 0, other, mine)
        parts = [first[:half, :], second[:half, :], first[half:, :], second[half:, :]]
        out_ref[...] = jnp.concatenate(parts, axis=0)


def potential_kernel(parts_ref, own_potential_ref, potential_ref, out_ref):
    summed = jnp.sum(parts_ref[...].astype(f32), axis=0)
    count = potential_ref.shape[0]
    rows = summed.shape[0] // (2 * count)
    half = rows // 2
    low = lax.broadcasted_iota(jnp.int32, (64, 128), 1) < 64
    results = []
    for pair in range(2 * count):
        source = own_potential_ref if pair < count else potential_ref
        blocks = []
        for part in range(2):
            matrices = source[pair % count, part].astype(f32)
            blocks.append(jnp.where(low, matrices, 0.0))
            blocks.append(jnp.where(low, 0.0, matrices))
        weights = jnp.concatenate(blocks, axis=0).astype(bf16)
        high, middle, lowest = three_parts(summed[pair * rows : (pair + 1) * rows, :])
        pieces = jnp.concatenate(
            [high.astype(f32), middle.astype(f32), lowest.astype(f32)], axis=0
        ).astype(bf16)
        product = dot(pieces, weights, NT)
        product = product[2 * rows :, :] + product[rows : 2 * rows, :] + product[:rows, :]
        real, imag = product[:, :128], product[:, 128:]
        results.append(real[:half, :] - imag[half:, :])
        results.append(real[half:, :] + imag[:half, :])
    applied = jnp.concatenate(results, axis=0).astype(bf16)
    out_ref[...] = jnp.broadcast_to(applied[None], out_ref.shape)


def return_kernel(
    applied_ref, own_template_ref, template_ref, own_cos_ref, own_sin_ref, cos_ref, sin_ref,
    select_ref, out_ref, stack_ref,
):
    atoms = cos_ref.shape[0]
    _, rows, waves = out_ref.shape
    half = rows // 2
    weights = [double_weights(own_template_ref[...]), double_weights(template_ref[...])]
    low = lax.broadcasted_iota(jnp.int32, (1, 128), 1) < 64
    zero = jnp.zeros((rows, waves), f32)

    def step(block, carry):
        base = pl.multiple_of(block * CHUNK, CHUNK)
        chunk = pl.ds(base, CHUNK)
        size = CHUNK // 2
        select = select_ref[pl.ds(pl.multiple_of(block * size, size), size), :]
        height = size * rows
        whole = applied_ref[pl.ds(pl.multiple_of(base // 2 * rows, height), height), :]
        whole = whole.astype(f32)
        for pair in range(size):
            applied = whole[pair * rows : (pair + 1) * rows, :]
            chosen = select[pair : pair + 1, :] > 0.5
            two = slice(2 * pair * rows, 2 * (pair + 1) * rows)
            for kind in range(2):
                take_even = low & chosen if kind == 0 else low & ~chosen
                take_odd = ~low & ~chosen if kind == 0 else ~low & chosen
                split = jnp.concatenate(
                    [jnp.where(take_even, applied, 0.0), jnp.where(take_odd, applied, 0.0)], axis=0
                )
                stack_ref[two, kind * 128 : (kind + 1) * 128] = split.astype(bf16)
        sums = []
        for side, (cosines, sines) in enumerate(((own_cos_ref, own_sin_ref), (cos_ref, sin_ref))):
            straight, turned = carry[side]
            cosine, sine = cosines[chunk, :], sines[chunk, :]
            images = dot(stack_ref[...], weights[side], NN)
            for atom in range(CHUNK):
                image = images[atom * rows : (atom + 1) * rows, :]
                straight = straight + cosine[atom : atom + 1, :] * image
                turned = turned + sine[atom : atom + 1, :] * image
            sums.append((straight, turned))
        return tuple(sums)

    sums = lax.fori_loop(0, atoms // CHUNK, step, ((zero, zero), (zero, zero)))
    for side, (straight, turned) in enumerate(sums):
        real = straight[:half, :] + turned[half:, :]
        imag = straight[half:, :] - turned[:half, :]
        out_ref[side] = jnp.concatenate([real, imag], axis=0)


def vmem(count):
    return [pl.BlockSpec(memory_space=pltpu.VMEM)] * count


def shape(dims, dtype):
    return jax.ShapeDtypeStruct(dims, dtype)


def call(kernel, args, out_shape, scratch_shapes=(), unread=0):
    return pl.pallas_call(
        kernel,
        in_specs=vmem(len(args) - unread) + [pl.BlockSpec(memory_space=pltpu.HBM)] * unread,
        out_specs=tuple(vmem(len(out_shape))),
        out_shape=tuple(out_shape),
        scratch_shapes=scratch_shapes,
        compiler_params=LIMIT,
    )(*args)


def flip(array, *axes):
    pairs = [(place, 2 ** len(axes) - 1 - place) for place in range(2 ** len(axes))]
    return lax.ppermute(array, axes, pairs)


def per_device(bands_in, template, potential, miller, positions, species, atom_order, reciprocal):
    plane = lax.axis_size("z") * lax.axis_size("x")
    groups = lax.axis_size("yh") * lax.axis_size("core")
    slot_dev = potential.shape[0]
    atoms = 2 * slot_dev * plane
    species_count, harmonics, waves = template.shape
    bands = bands_in.shape[1]
    rows = bands
    pairs = slot_dev // 2
    message = 2 * pairs * rows
    width = 2 * harmonics
    template = template.reshape(species_count * harmonics, waves)
    fields = bands_in.reshape(2 * bands, waves)
    matrices = potential.reshape(pairs, 2, 2, harmonics, harmonics)
    matrices = matrices.transpose(0, 2, 3, 1, 4).reshape(pairs, 2, harmonics, width)
    core = lax.axis_index("core")
    stride = groups * slot_dev
    first_slot = lax.axis_index("yl") * plane * stride + lax.axis_index("yh") * 2 * slot_dev
    place = jnp.stack([first_slot, core]).astype(jnp.int32).reshape(1, 2)
    lengths = reciprocal.reshape(1, 3)
    coefs_shape = shape((atoms // 2 * rows, width), bf16)
    fields_shape = shape((rows, waves), f32)
    whole_shape = shape((2 * bands, waves), f32)
    phase_shape = shape((atoms, waves), f32)
    kinetic_shape = shape((1, waves), f32)
    weights_shape = shape((2 * width, waves), bf16)
    wave_scratch = pltpu.VMEM((2, CHUNK * rows, waves), bf16)

    other_miller = flip(miller, "yl")
    other_fields = flip(fields, "yl")
    other_template = flip(template, "yl")
    inputs = (
        atom_order.reshape(1, -1), positions, species.reshape(1, -1), miller, lengths, fields,
        template,
    )
    inputs = tuple(pltpu.with_memory_space_constraint(value, pltpu.HBM) for value in inputs)
    own_cos, own_sin, select, table, own, own_kinetic, own_both, lengths = call(
        functools.partial(prepare_kernel, stride, slot_dev),
        (place,) + inputs,
        (
            phase_shape, phase_shape, shape((atoms // 2, 128), f32), shape((atoms, 16), f32),
            fields_shape, kinetic_shape, weights_shape, shape(lengths.shape, f32),
        ),
        [pltpu.VMEM(value.shape, value.dtype) for value in inputs]
        + [pltpu.SemaphoreType.DMA((len(inputs),))],
        unread=len(inputs),
    )
    coefs, other_cos, other_sin, other, other_kinetic, other_both = call(
        first_kernel,
        (
            place, lengths, table, other_miller, own, other_fields, own_both, other_template,
            own_cos, own_sin, select,
        ),
        (
            coefs_shape, phase_shape, phase_shape, fields_shape, kinetic_shape, weights_shape,
        ),
        [wave_scratch],
    )
    other_matrices = flip(matrices, "core")
    phases = (own_cos, own_sin, other_cos, other_sin, select)

    def return_fields(coefs):
        parts = lax.all_to_all(coefs.reshape(plane, message, width), ("x", "z"), 0, 0, tiled=True)
        (applied,) = call(
            potential_kernel,
            (parts, matrices, other_matrices),
            (shape((plane, message, width), bf16),),
        )
        applied = lax.all_to_all(applied, ("x", "z"), 0, 0, tiled=True)
        (mine,) = call(
            return_kernel,
            (applied.reshape(atoms // 2 * rows, width), template, other_template) + phases,
            (shape((2, rows, waves), f32),),
            [pltpu.VMEM((CHUNK * rows, 2 * width), bf16)],
        )
        return mine

    def around(same, turned):
        low = flip(turned, "yl")
        both = flip(turned, "yl", "yh")
        high = flip(same, "yh")
        return low, high, both

    mine = return_fields(coefs)
    once, coefs = call(
        next_kernel,
        (own_kinetic, other_kinetic, own, other, mine)
        + around(mine, mine)
        + (own_both, other_both)
        + phases,
        (fields_shape, coefs_shape),
        [wave_scratch],
    )
    mine = return_fields(coefs)
    (mine,) = call(
        last_kernel,
        (own_kinetic, once, mine) + around(mine[0], mine[1]),
        (shape((2, rows, waves), f32),),
    )
    once, twice = call(join_kernel, (place, mine, flip(mine, "core")), (whole_shape, whole_shape))
    return once.reshape(bands_in.shape), twice.reshape(bands_in.shape)


def solution(mesh):
    pw, groups = mesh.devices.shape
    fine = Mesh(
        mesh.devices.reshape(2, 8, pw // 16, 2, groups // 2), ("yl", "z", "x", "yh", "core")
    )
    waves, slots = ("yl", "z", "x"), ("yl", "z", "x", "yh", "core")
    in_specs = (
        P(None, None, waves),
        P(None, None, waves),
        P(slots, None),
        P(None, waves),
        P(),
        P(),
        P(),
        P(),
    )
    out_specs = (P(None, None, waves), P(None, None, waves))

    return jax.shard_map(
        per_device, mesh=fine, in_specs=in_specs, out_specs=out_specs, check_vma=False
    )
```
